32 devices in a mesh: parts: 2 (over y), seq: 4 (over z), head: 4 (over x, core).
Axes of the slice: x: 2, y: 2, z: 4, core: 2. Of those that a mesh axis runs over, the one named last changes fastest.
Arguments:
- query_raw: bfloat16 [6144, 4096], P(('parts', 'seq'), 'head'), parts along dimension 0, may hold values from -6 to 6
- key_raw: bfloat16 [6144, 4096], P(('parts', 'seq'), 'head'), parts along dimension 0, may hold values from -18 to 18
- value_raw: bfloat16 [6144, 4096], P(('parts', 'seq'), 'head'), parts along dimension 0, may hold values from -6 to 6
- out_gate: bfloat16 [6144, 4096], P(('parts', 'seq'), 'head'), parts along dimension 0, may hold values from -6 to 6
- log_decay: float32 [32, 6144], P('head', ('parts', 'seq')), parts along dimension 1, may hold values from -1.2 to 0
- write_strength: float32 [32, 6144], P('head', ('parts', 'seq')), parts along dimension 1, may hold values from 0 to 1
- conv_weight: float32 [3, 4, 4096], P(None, None, 'head'), may hold values from -3 to 3
- norm_gain: float32 [128], replicated, may hold values from 0.25 to 1.75
- out_weight: bfloat16 [4096, 2304], P('head'), may hold values from -0.09375 to 0.09375
- history_end: int32 [2], P('parts'), parts along dimension 0, may hold values from 1536 to 3072
Outputs:
- layer_out: bfloat16 [6144, 2304], P(('parts', 'seq', 'head')), parts along dimension 0
The draws below stay inside these ranges and needn't reach their ends.
There are 2 independent parts, one for each index of `parts`. The reference program is written for one: setup_inputs(seed, part) draws one part's arguments, and reference() takes and returns one part's arrays. A program takes and returns all parts, laid end to end along the dimension named above; an argument that names none is the same for every part. Nothing has to cross between parts.
Inputs may be any that keep to these rules, and one draw needn't show every extreme that they name: Positions at and after history_end[0] are padding.
All inputs are finite; a program needn't handle non-finite values.
Results may differ from the reference program's by a relative error of at most 0.014.
Values may be sent and summed in bfloat16 or wider, within the bound.
No kernel may reach another device: no remote copies, remote signals or barrier semaphores. Data moves between devices by JAX's collectives and lax.ppermute only.
A program may use at most 192 MiB of HBM per device.

```python
import math
import jax
import jax.numpy as jnp
from jax import lax

D = 2304
HEAD_TOTAL = 32
DK = 128
TOK_DEV = 768
HK = 4096
TOKENS = 3072
GROUPS = 4


def slow_heads(key, keep_count):
    return jax.random.randint(jax.random.fold_in(key, 11), (HEAD_TOTAL,), 0, 10) < keep_count


def spread_log(key, shape, lower, upper):
    return jnp.exp(jax.random.uniform(key, shape, jnp.float32, math.log(lower), math.log(upper)))


def draw_key_raw(key, part):
    channel_scale = spread_log(jax.random.fold_in(key, 41), (1, HK), 0.15, 3.0)
    base = jnp.clip(jax.random.normal(jax.random.fold_in(key, 42), (TOKENS, HK), jnp.float32), -6.0, 6.0)
    return (base * channel_scale).astype(jnp.bfloat16)


def draw_log_decay(key, part):
    slow_set = slow_heads(key, 5)
    random_wobble = 1.0 + 0.25 * jnp.clip(jax.random.normal(jax.random.fold_in(key, 24), (HEAD_TOTAL, TOKENS), jnp.float32), -2.0, 2.0)
    slow_rate = spread_log(jax.random.fold_in(key, 21), (HEAD_TOTAL, 1), 0.05, 0.2) * (math.log(10.0) / TOKENS)
    fast_rate = spread_log(jax.random.fold_in(key, 22), (HEAD_TOTAL, 1), 1.0 / 60.0, 1.0 / 25.0)
    fading_speed = jnp.where(slow_set[:, None], slow_rate, fast_rate)
    block_count = TOKENS // TOK_DEV
    multiplier = jnp.repeat(spread_log(jax.random.fold_in(key, 23), (HEAD_TOTAL, block_count), 0.5, 2.0), TOK_DEV, axis=1)
    places = jax.random.randint(jax.random.fold_in(key, 25), (HEAD_TOTAL, 2), 0, TOKENS)
    surge_depth = jax.random.uniform(jax.random.fold_in(key, 26), (HEAD_TOTAL, 2), jnp.float32, 0.22, 0.5)
    agreement_flags = jnp.arange(TOKENS, dtype=jnp.int32)[None, None, :] == places[:, :, None]
    surge_events = jnp.sum(jnp.where(agreement_flags, surge_depth[:, :, None], 0.0), axis=1)
    return (-(fading_speed * multiplier * random_wobble + surge_events)).astype(jnp.float32)


def draw_write_strength(key, part):
    slow_set = slow_heads(key, 5)
    slow_write = jax.random.uniform(jax.random.fold_in(key, 31), (HEAD_TOTAL, TOKENS), jnp.float32, 0.02, 0.1)
    fast_write = jax.random.uniform(jax.random.fold_in(key, 32), (HEAD_TOTAL, TOKENS), jnp.float32, 0.1, 0.9)
    return jnp.where(slow_set[:, None], slow_write, fast_write).astype(jnp.float32)


def level_of(rng, extent, cuts, smallest, high):
    def one(axis_at, blocks):
        steps = jax.random.uniform(jax.random.fold_in(jax.random.fold_in(rng, 6), axis_at), (blocks,), jnp.float32, smallest / len(cuts), high / len(cuts))
        return jnp.repeat(jnp.exp(steps), extent[axis_at] // blocks).reshape((-1,) + (1,) * (len(extent) - axis_at - 1))

    loudness = one(*cuts[0])
    for cut in cuts[1:]:
        loudness = loudness * one(*cut)
    return loudness


def normal_values(own_key, shape, spread, limit, split=(), kind=jnp.bfloat16):
    result = spread * jax.random.normal(own_key, shape, jnp.float32)
    if split:
        result = result * level_of(own_key, shape, split, -0.22, 0.18)
    return jnp.clip(result, -limit, limit).astype(kind)


def setup_inputs(seed: int = 0, part: int = 0) -> dict:
    splits = jax.random.split(jax.random.key(seed), 11)
    part_splits = jax.random.split(jax.random.fold_in(splits[10], part), 11)
    return {
        "query_raw": normal_values(part_splits[0], (TOKENS, HK), 1.0, 6.0, ((0, 4), (1, 4))),
        "key_raw": draw_key_raw(jax.random.fold_in(jax.random.fold_in(splits[10], part), 71), part),
        "value_raw": normal_values(part_splits[2], (TOKENS, HK), 1.0, 6.0, ((0, 4), (1, 4))),
        "out_gate": normal_values(part_splits[3], (TOKENS, HK), 1.0, 6.0, ((0, 4), (1, 4))),
        "log_decay": draw_log_decay(jax.random.fold_in(jax.random.fold_in(splits[10], part), 71), part),
        "write_strength": draw_write_strength(jax.random.fold_in(jax.random.fold_in(splits[10], part), 71), part),
        "conv_weight": normal_values(splits[6], (3, 4, HK), 4 ** -0.5, 3.0, ((2, 4),), jnp.float32),
        "norm_gain": jnp.clip(1.0 + 0.15 * jax.random.normal(splits[7], (DK,), jnp.float32), 0.25, 1.75),
        "out_weight": normal_values(splits[8], (HK, D), HK ** -0.5, 0.09375, ((0, 4),)),
        "history_end": jax.random.randint(part_splits[9], (1,), TOKENS // 2, TOKENS + 1).astype(jnp.int32),
    }


block_len = 64

def exact_einsum(form, left, right):
    return jnp.einsum(form, left, right, precision=lax.Precision.HIGHEST)

def conv_silu(raw_rows, rim_rows, taps):
    rows_total = raw_rows.shape[0]
    padded = jnp.concatenate([rim_rows, raw_rows], axis=0).astype(jnp.float32)
    summed = taps[0] * padded[0:rows_total]
    for tap_index in range(1, 4):
        summed = summed + taps[tap_index] * padded[tap_index:tap_index + rows_total]
    return jax.nn.silu(summed)

def unit_heads(values, head_width, multiplier):
    shaped = values.reshape(values.shape[0], -1, head_width)
    norms = lax.rsqrt(lax.optimization_barrier(jnp.sum(shaped * shaped, axis=-1, keepdims=True)) + 1e-06)
    return (shaped * norms * multiplier).reshape(values.shape).astype(jnp.bfloat16)

def stretch_terms(queries, keys, values, decays, writes):
    span = decays.shape[-1]
    cumulative = jnp.cumsum(decays, axis=-1)
    gammas = jnp.exp(cumulative)
    log_gaps = cumulative[:, :, None] - cumulative[:, None, :]
    row_ids = lax.broadcasted_iota(jnp.int32, (span, span), 0)
    col_ids = lax.broadcasted_iota(jnp.int32, (span, span), 1)
    inclusive = col_ids <= row_ids
    strict = col_ids < row_ids
    decay_incl = jnp.where(inclusive, jnp.exp(jnp.where(inclusive, log_gaps, 0.0)), 0.0)
    decay_strict = jnp.where(strict, decay_incl, 0.0)
    key_gram = exact_einsum('hid,hjd->hij', keys, keys)
    system = jnp.eye(span, dtype=jnp.float32) + writes[:, :, None] * key_gram * decay_strict
    key_mix = jax.scipy.linalg.solve_triangular(system, (writes * gammas)[:, :, None] * keys, lower=True, unit_diagonal=True)
    value_mix = jax.scipy.linalg.solve_triangular(system, writes[:, :, None] * values, lower=True, unit_diagonal=True)
    scores = exact_einsum('hid,hjd->hij', queries, keys) * decay_incl
    last_decay = gammas[:, -1]
    keys_out = keys * jnp.exp(cumulative[:, -1:] - cumulative)[:, :, None]
    return (gammas, key_mix, value_mix, scores, last_decay, keys_out)

def reference(query_raw, key_raw, value_raw, out_gate, log_decay, write_strength, conv_weight, norm_gain, out_weight, history_end):
    rim_zero = jnp.zeros((3, HK), jnp.bfloat16)
    queries = unit_heads(conv_silu(query_raw, rim_zero, conv_weight[0]), DK, DK ** (-0.5))
    keys_all = unit_heads(conv_silu(key_raw, rim_zero, conv_weight[1]), DK, 1.0)
    values_all = conv_silu(value_raw, rim_zero, conv_weight[2]).astype(jnp.bfloat16)
    stretch_count = TOKENS // block_len

    def by_stretch(array):
        return array.reshape(stretch_count, block_len, HEAD_TOTAL, DK)

    def gate_stretches(array):
        return array.reshape(HEAD_TOTAL, stretch_count, block_len).transpose(1, 0, 2)

    def stretch_step(state, block_inputs):
        query_block, key_block, value_block, decay_block, write_block = block_inputs
        query_f = query_block.astype(jnp.float32).transpose(1, 0, 2)
        key_f = key_block.astype(jnp.float32).transpose(1, 0, 2)
        value_f = value_block.astype(jnp.float32).transpose(1, 0, 2)
        gammas, key_mix, value_mix, scores, last_decay, keys_out = stretch_terms(query_f, key_f, value_f, decay_block, write_block)
        fresh = value_mix - exact_einsum('hcd,hde->hce', key_mix, state)
        output = gammas[:, :, None] * exact_einsum('hcd,hde->hce', query_f, state) + exact_einsum('hij,hje->hie', scores, fresh)
        new_state = last_decay[:, None, None] * state + exact_einsum('hcd,hce->hde', keys_out, fresh)
        return (new_state, output)
    start_state = jnp.zeros((HEAD_TOTAL, DK, DK), jnp.float32)
    final_state, outputs = lax.scan(stretch_step, start_state, (by_stretch(queries), by_stretch(keys_all), by_stretch(values_all), gate_stretches(log_decay), gate_stretches(write_strength)))
    mixed_heads = outputs.transpose(0, 2, 1, 3).reshape(TOKENS, HEAD_TOTAL, DK)
    normed = mixed_heads * lax.rsqrt(lax.optimization_barrier(jnp.mean(mixed_heads * mixed_heads, axis=-1, keepdims=True)) + 1e-06) * norm_gain
    gated = normed.reshape(TOKENS, HK) * jax.nn.silu(out_gate.astype(jnp.float32))
    positions = jnp.arange(TOKENS, dtype=jnp.int32)
    gated = jnp.where((positions < history_end[0])[:, None], gated, 0.0).astype(jnp.bfloat16)
    group_span = HK // GROUPS
    total = jnp.zeros((TOKENS, D), jnp.float32)
    for group_index in range(GROUPS):
        lower_edge = group_index * group_span
        partial_prod = jnp.dot(gated[:, lower_edge:lower_edge + group_span].astype(jnp.float32), out_weight[lower_edge:lower_edge + group_span].astype(jnp.float32), preferred_element_type=jnp.float32).astype(jnp.bfloat16)
        partial_prod = lax.optimization_barrier(partial_prod)
        total = total + partial_prod.astype(jnp.float32)
    return total.astype(jnp.bfloat16)
```

```python
import jax
import jax.numpy as jnp
from jax import lax
from jax.experimental import pallas as pl
from jax.experimental.pallas import tpu as pltpu
from jax.sharding import PartitionSpec as P

CHUNK = 128
RIM = 16
INV_PASSES = 1
F32 = jnp.float32
BF16 = jnp.bfloat16
NN = (((1,), (0,)), ((), ()))
NT = (((1,), (1,)), ((), ()))


def mm(left, right, dims=NN):
    return lax.dot_general(left, right, dims, preferred_element_type=F32)


def exact(left, right, dims=NN):
    return lax.dot_general(
        left, right, dims, precision=lax.Precision.HIGHEST, preferred_element_type=F32
    )


def halves(x):
    high = x.astype(BF16)
    return high, (x - high.astype(F32)).astype(BF16)


def mm3(left, right):
    if INV_PASSES == 1:
        return mm(left.astype(BF16), right.astype(BF16))
    if INV_PASSES == 6:
        return exact(left, right)
    lh, ll = halves(left)
    rh, rl = halves(right)
    return mm(
        jnp.concatenate([lh, ll], axis=1), jnp.concatenate([rh, rh], axis=0)
    ) + mm(lh, rl)


def conv_silu(raw, rim, taps):
    rows = raw.shape[0]
    padded = jnp.concatenate([rim, raw], axis=0)
    n = rim.shape[0]
    total = taps[3:4] * raw
    for j in range(3):
        total = total + taps[j : j + 1] * padded[n - 3 + j : n - 3 + j + rows]
    return total * (1.0 / (1.0 + jnp.exp(-total)))


def chunk_kernel(
    rim_ref, q_ref, k_ref, v_ref, qp_ref, kp_ref, vp_ref, dec_ref, wr_ref, taps_ref,
    local_ref, qeff_ref, summary_ref, state_ref,
):
    step = pl.program_id(0)
    c = q_ref.shape[0]
    heads = dec_ref.shape[0]
    width = q_ref.shape[1] // heads

    @pl.when(step == 0)
    def _():
        rows = lax.broadcasted_iota(jnp.int32, (width, 2 * width), 0)
        cols = lax.broadcasted_iota(jnp.int32, (width, 2 * width), 1)
        eye = jnp.where(rows == cols, 1.0, 0.0).astype(F32)
        for h in range(heads):
            state_ref[h] = eye

    ri = lax.broadcasted_iota(jnp.int32, (c, c), 0)
    ci = lax.broadcasted_iota(jnp.int32, (c, c), 1)
    tril = jnp.where(ci <= ri, 1.0, 0.0).astype(F32)
    eye = jnp.where(ci == ri, 1.0, 0.0).astype(F32)
    strict = ci < ri
    inclusive = ci <= ri
    differ = ri ^ ci
    dec = dec_ref[...]
    wr = wr_ref[...]
    cum_row = exact(dec, tril, NT)
    cum_col = exact(tril, dec, NT)
    wr_col = exact(eye, wr, NT)
    last = cum_row[:, c - 1 : c]
    gamma_row = jnp.exp(cum_row)
    gamma_col = jnp.exp(cum_col)
    kout_row = jnp.exp(last - cum_row)
    last_decay = jnp.exp(last)
    first = step == 0

    def channels(ref, prev_ref, which, h):
        sl = slice(h * width, (h + 1) * width)
        raw = ref[:, sl].astype(F32)
        rim = jnp.where(
            first, rim_ref[which, :, sl].astype(F32), prev_ref[:, sl].astype(F32)
        )
        return conv_silu(raw, rim[-8:], taps_ref[which, :, sl])

    for h in range(heads):
        sl = slice(h * width, (h + 1) * width)
        q = channels(q_ref, qp_ref, 0, h)
        k = channels(k_ref, kp_ref, 1, h)
        v = channels(v_ref, vp_ref, 2, h).astype(BF16)
        q = (q * (lax.rsqrt(jnp.sum(q * q, axis=-1, keepdims=True) + 1e-06) * width ** -0.5)).astype(BF16)
        k = (k * lax.rsqrt(jnp.sum(k * k, axis=-1, keepdims=True) + 1e-06)).astype(BF16)
        grams = mm(jnp.concatenate([q, k], axis=0), k, NT)
        gap = cum_col[:, h : h + 1] - cum_row[h : h + 1, :]
        decay = jnp.exp(jnp.minimum(gap, 0.0))
        scores = jnp.where(inclusive, grams[:c] * decay, 0.0).astype(BF16)
        low = jnp.where(strict, grams[c:] * decay * wr_col[:, h : h + 1], 0.0)
        inv = eye - jnp.where(differ == 1, low, 0.0)
        size = 2
        while size < c:
            part = jnp.where((differ >= size) & (differ < 2 * size), low, 0.0)
            inv = inv - mm3(inv, mm3(part, inv))
            size *= 2
        wr_r = wr[h : h + 1, :]
        key_mix = mm((inv * (wr_r * gamma_row[h : h + 1, :])).astype(BF16), k)
        value_mix = mm((inv * wr_r).astype(BF16), v)
        kf = k.astype(F32)
        q_in = (q.astype(F32) * gamma_col[:, h : h + 1]).astype(BF16)
        k_out = (kf.T * kout_row[h : h + 1, :]).astype(BF16)
        state = state_ref[h]
        read = mm(jnp.concatenate([key_mix.astype(BF16), q_in], axis=0), state.astype(BF16))
        fresh = jnp.concatenate(
            [-read[:c, :width], value_mix - read[:c, width:]], axis=1
        ).astype(BF16)
        both = mm(jnp.concatenate([scores, k_out], axis=0), fresh)
        out = read[c:] + both[:c]
        qeff_ref[:, sl] = out[:, :width].astype(BF16)
        local_ref[:, sl] = out[:, width:]
        state = last_decay[h : h + 1, :] * state + both[c:]
        state_ref[h] = state

    @pl.when(step == pl.num_programs(0) - 1)
    def _():
        summary_ref[...] = state_ref[...].astype(BF16)


def finish_kernel(
    info_ref, all_ref, local_ref, qeff_ref, gate_ref, gain_ref, weight_ref, out_ref, state_ref
):
    step = pl.program_id(0)
    count = pl.num_programs(0) - info_ref[2]
    heads, width = state_ref.shape[0], state_ref.shape[1]
    rows = local_ref.shape[0]

    @pl.when(step == 0)
    def _():
        state_ref[...] = jnp.zeros(state_ref.shape, F32)

    @pl.when(step < info_ref[0])
    def _():
        for h in range(heads):
            state_ref[h] = (
                mm(all_ref[0, h, :, :width], state_ref[h].astype(BF16))
                + all_ref[0, h, :, width:].astype(F32)
            )

    @pl.when(step >= count)
    def _():
        base = info_ref[1] + (step - count) * rows
        pos = base + lax.broadcasted_iota(jnp.int32, (rows, width), 0)
        valid = pos < info_ref[3]
        gated = []
        for h in range(heads):
            sl = slice(h * width, (h + 1) * width)
            o = local_ref[:, sl] + mm(qeff_ref[:, sl], state_ref[h].astype(BF16))
            norm = lax.rsqrt(jnp.mean(o * o, axis=-1, keepdims=True) + 1e-06)
            g = gate_ref[:, sl].astype(F32)
            o = o * norm * gain_ref[...] * (g * (1.0 / (1.0 + jnp.exp(-g))))
            gated.append(jnp.where(valid, o, 0.0).astype(BF16))
        out_ref[...] = mm(jnp.concatenate(gated, axis=1), weight_ref[...]).astype(BF16)


def passed_along(block, axis, distance):
    devices = range(lax.axis_size(axis))
    route = [(i - distance, i) for i in devices if i - distance in devices]
    return lax.ppermute(block, axis, route)


def on_device(
    query_raw, key_raw, value_raw, out_gate, log_decay, write_strength,
    conv_weight, norm_gain, out_weight, history_end,
):
    rows, channels = query_raw.shape
    heads = log_decay.shape[0]
    width = channels // heads
    c = CHUNK
    steps = rows // c
    rim = passed_along(
        jnp.stack([query_raw[-RIM:], key_raw[-RIM:], value_raw[-RIM:]]), "seq", 1
    )
    per = c // RIM
    block = pl.BlockSpec((c, channels), lambda i: (i, 0))
    prev = pl.BlockSpec((RIM, channels), lambda i: (jnp.maximum(i * per - 1, 0), 0))
    gates = pl.BlockSpec((heads, c), lambda i: (0, i))
    local, qeff, summary = pl.pallas_call(
        chunk_kernel,
        grid=(steps,),
        in_specs=[
            pl.BlockSpec((3, RIM, channels), lambda i: (0, 0, 0)),
            block, block, block, prev, prev, prev, gates, gates,
            pl.BlockSpec((3, 4, channels), lambda i: (0, 0, 0)),
        ],
        out_specs=[
            block, block,
            pl.BlockSpec((heads, width, 2 * width), lambda i: (0, 0, 0)),
        ],
        out_shape=[
            jax.ShapeDtypeStruct((rows, channels), F32),
            jax.ShapeDtypeStruct((rows, channels), BF16),
            jax.ShapeDtypeStruct((heads, width, 2 * width), BF16),
        ],
        scratch_shapes=[pltpu.VMEM((heads, width, 2 * width), F32)],
        compiler_params=pltpu.CompilerParams(vmem_limit_bytes=48 << 20),
        name="chunks",
    )(rim, query_raw, key_raw, value_raw, query_raw, key_raw, value_raw,
      log_decay, write_strength, conv_weight)
    count = lax.axis_size("seq")
    place = lax.axis_index("seq")
    gathered = lax.all_gather(summary, "seq")
    dim = out_weight.shape[1]
    tile = 256
    tiles = rows // tile
    info = jnp.stack([place, place * rows, tiles, history_end[0]]).astype(jnp.int32)
    row_block = lambda i, s: (jnp.maximum(i - count, 0), 0)
    partial = pl.pallas_call(
        finish_kernel,
        grid_spec=pltpu.PrefetchScalarGridSpec(
            num_scalar_prefetch=1,
            grid=(count + tiles,),
            in_specs=[
                pl.BlockSpec((1, heads, width, 2 * width), lambda i, s: (jnp.minimum(i, count - 1), 0, 0, 0)),
                pl.BlockSpec((tile, channels), row_block),
                pl.BlockSpec((tile, channels), row_block),
                pl.BlockSpec((tile, channels), row_block),
                pl.BlockSpec((1, width), lambda i, s: (0, 0)),
                pl.BlockSpec((channels, dim), lambda i, s: (0, 0)),
            ],
            out_specs=pl.BlockSpec((tile, dim), row_block),
            scratch_shapes=[pltpu.VMEM((heads, width, width), F32)],
        ),
        out_shape=jax.ShapeDtypeStruct((rows, dim), BF16),
        compiler_params=pltpu.CompilerParams(vmem_limit_bytes=48 << 20),
        name="finish",
    )(info, gathered, local, qeff, out_gate, norm_gain.reshape(1, width), out_weight)
    return lax.psum_scatter(partial, "head", scatter_dimension=0, tiled=True)


def solution(mesh):
    return jax.shard_map(
        on_device,
        mesh=mesh,
        in_specs=(
            P(("parts", "seq"), "head"),
            P(("parts", "seq"), "head"),
            P(("parts", "seq"), "head"),
            P(("parts", "seq"), "head"),
            P("head", ("parts", "seq")),
            P("head", ("parts", "seq")),
            P(None, None, "head"),
            P(),
            P("head", None),
            P("parts"),
        ),
        out_specs=P(("parts", "seq", "head"), None),
        check_vma=False,
    )
```

```python
import jax
import jax.numpy as jnp
import numpy as np
from jax import lax
from jax.experimental import pallas as pl
from jax.experimental.pallas import tpu as pltpu
from jax.sharding import PartitionSpec as P

CHUNK = 128
RIM = 16
GROUP = 8
F32 = jnp.float32
BF16 = jnp.bfloat16
NN = (((1,), (0,)), ((), ()))
NT = (((1,), (1,)), ((), ()))


def mm(left, right, dims=NN):
    return lax.dot_general(left, right, dims, preferred_element_type=F32)


def exact(left, right, dims=NN):
    return lax.dot_general(
        left, right, dims, precision=lax.Precision.HIGHEST, preferred_element_type=F32
    )


def sigmoid(x):
    return 1.0 / (1.0 + jnp.exp(-x))


def conv_silu(raw, rim, taps):
    rows = raw.shape[0]
    padded = jnp.concatenate([rim, raw], axis=0)
    n = rim.shape[0]
    total = taps[3:4] * raw
    for j in range(3):
        total = total + taps[j : j + 1] * padded[n - 3 + j : n - 3 + j + rows]
    return total * sigmoid(total)


def unit(x, scale):
    return (x * (lax.rsqrt(jnp.sum(x * x, axis=-1, keepdims=True) + 1e-06) * scale)).astype(BF16)


def positions(c):
    return (
        lax.broadcasted_iota(jnp.int32, (c, c), 0),
        lax.broadcasted_iota(jnp.int32, (c, c), 1),
    )


def channels(rim_ref, ref, prev_ref, taps_ref, which, sl, first):
    raw = ref[:, sl].astype(F32)
    rim = jnp.where(first, rim_ref[which, :, sl].astype(F32), prev_ref[:, sl].astype(F32))
    return conv_silu(raw, rim[-8:], taps_ref[which, :, sl])


def summary_kernel(
    rim_ref, k_ref, v_ref, kp_ref, vp_ref, dec_ref, wr_ref, taps_ref, mask_ref,
    keys_ref, fresh_ref, start_ref, summary_ref, state_ref,
):
    step = pl.program_id(0)
    c = k_ref.shape[0]
    heads = dec_ref.shape[0]
    width = k_ref.shape[1] // heads

    @pl.when(step == 0)
    def _():
        rows = lax.broadcasted_iota(jnp.int32, (width, 2 * width), 0)
        cols = lax.broadcasted_iota(jnp.int32, (width, 2 * width), 1)
        eye = jnp.where(rows == cols, 1.0, 0.0).astype(F32)
        for h in range(heads):
            state_ref[h] = eye

    ri, ci = positions(c)
    tril = jnp.where(ci <= ri, 1.0, 0.0).astype(F32)
    eye = jnp.where(ci == ri, 1.0, 0.0).astype(F32)
    dec = dec_ref[...]
    wr = wr_ref[...]
    cum_row = exact(dec, tril, NT)
    cum_col = exact(tril, dec, NT)
    wr_col = exact(eye, wr, NT)
    last = cum_row[:, c - 1 : c]
    wg_row = wr * jnp.exp(cum_row)
    kout_row = jnp.exp(last - cum_row)
    last_decay = jnp.exp(last)
    first = step == 0

    for g in range(0, heads, GROUP):
        hs = range(g, g + GROUP)
        sls = [slice(h * width, (h + 1) * width) for h in hs]
        n = range(GROUP)
        k = [unit(channels(rim_ref, k_ref, kp_ref, taps_ref, 1, sl, first), 1.0) for sl in sls]
        for i in n:
            keys_ref[:, sls[i]] = k[i]
        gram = [mm(x, x, NT) for x in k]
        low = []
        for i in n:
            h = hs[i]
            gap = cum_col[:, h : h + 1] - cum_row[h : h + 1, :]
            decay = jnp.exp(jnp.minimum(gap, 0.0)) * wr_col[:, h : h + 1]
            low.append(jnp.where(ci < ri, gram[i] * decay, 0.0).astype(BF16))
        inv = [eye - (x * mask_ref[0]).astype(F32) for x in low]
        level = 1
        while (1 << level) < c:
            mask = mask_ref[level]
            invb = [x.astype(BF16) for x in inv]
            inner = [mm(low[i] * mask, invb[i]).astype(BF16) for i in n]
            inv = [inv[i] - mm(invb[i], inner[i]) for i in n]
            level += 1
        v = [channels(rim_ref, v_ref, vp_ref, taps_ref, 2, sl, first).astype(BF16) for sl in sls]
        key_mix = [mm((inv[i] * wg_row[hs[i] : hs[i] + 1, :]).astype(BF16), k[i]).astype(BF16) for i in n]
        value_mix = [mm((inv[i] * wr[hs[i] : hs[i] + 1, :]).astype(BF16), v[i]) for i in n]
        k_out = [(k[i].astype(F32).T * kout_row[hs[i] : hs[i] + 1, :]).astype(BF16) for i in n]
        start = [state_ref[h].astype(BF16) for h in hs]
        for i in n:
            start_ref[0, hs[i]] = start[i]
        read = [mm(key_mix[i], start[i]) for i in n]
        fresh = [
            jnp.concatenate(
                [-read[i][:, :width], value_mix[i] - read[i][:, width:]], axis=1
            ).astype(BF16)
            for i in n
        ]
        for i in n:
            h = hs[i]
            fresh_ref[:, 2 * h * width : 2 * (h + 1) * width] = fresh[i]
        both = [mm(k_out[i], fresh[i]) for i in n]
        for i in n:
            h = hs[i]
            state_ref[h] = last_decay[h : h + 1, :] * state_ref[h] + both[i]

    @pl.when(step == pl.num_programs(0) - 1)
    def _():
        summary_ref[...] = state_ref[...].astype(BF16)


def local_kernel(
    rim_ref, q_ref, qp_ref, keys_ref, fresh_ref, start_ref, dec_ref, taps_ref,
    local_ref, qeff_ref,
):
    step = pl.program_id(0)
    c = q_ref.shape[0]
    heads = dec_ref.shape[0]
    width = q_ref.shape[1] // heads
    ri, ci = positions(c)
    tril = jnp.where(ci <= ri, 1.0, 0.0).astype(F32)
    dec = dec_ref[...]
    cum_row = exact(dec, tril, NT)
    cum_col = exact(tril, dec, NT)
    gamma_col = jnp.exp(cum_col)
    first = step == 0
    for g in range(0, heads, GROUP):
        hs = range(g, g + GROUP)
        sls = [slice(h * width, (h + 1) * width) for h in hs]
        n = range(GROUP)
        q = [unit(channels(rim_ref, q_ref, qp_ref, taps_ref, 0, sl, first), width ** -0.5) for sl in sls]
        gram = [mm(q[i], keys_ref[:, sls[i]], NT) for i in n]
        for i in n:
            h = hs[i]
            gap = cum_col[:, h : h + 1] - cum_row[h : h + 1, :]
            scores = jnp.where(ci <= ri, gram[i] * jnp.exp(jnp.minimum(gap, 0.0)), 0.0).astype(BF16)
            q_in = (q[i].astype(F32) * gamma_col[:, h : h + 1]).astype(BF16)
            out = mm(
                jnp.concatenate([q_in, scores], axis=1),
                jnp.concatenate(
                    [start_ref[0, h], fresh_ref[:, 2 * h * width : 2 * (h + 1) * width]], axis=0
                ),
            )
            qeff_ref[:, sls[i]] = out[:, :width].astype(BF16)
            local_ref[:, sls[i]] = out[:, width:]


def level_masks(c):
    r = np.arange(c)
    differ = r[:, None] ^ r[None, :]
    lower = r[:, None] > r[None, :]
    levels = []
    size = 1
    while size < c:
        levels.append(lower & (differ >= size) & (differ < 2 * size))
        size *= 2
    return jnp.asarray(np.stack(levels), BF16)


def front(rim, query_raw, key_raw, value_raw, log_decay, write_strength, conv_weight):
    rows, channel_count = query_raw.shape
    heads = log_decay.shape[0]
    width = channel_count // heads
    c = CHUNK
    steps = rows // c
    per = c // RIM
    masks = level_masks(c)
    block = pl.BlockSpec((c, channel_count), lambda i: (i, 0))
    wide = pl.BlockSpec((c, 2 * channel_count), lambda i: (i, 0))
    prev = pl.BlockSpec((RIM, channel_count), lambda i: (jnp.maximum(i * per - 1, 0), 0))
    gates = pl.BlockSpec((heads, c), lambda i: (0, i))
    rims = pl.BlockSpec((3, RIM, channel_count), lambda i: (0, 0, 0))
    taps = pl.BlockSpec((3, 4, channel_count), lambda i: (0, 0, 0))
    starts = pl.BlockSpec((1, heads, width, 2 * width), lambda i: (i, 0, 0, 0))
    params = pltpu.CompilerParams(vmem_limit_bytes=48 << 20)
    keys, fresh, start, summary = pl.pallas_call(
        summary_kernel,
        grid=(steps,),
        in_specs=[
            rims, block, block, prev, prev, gates, gates, taps,
            pl.BlockSpec(masks.shape, lambda i: (0, 0, 0)),
        ],
        out_specs=[
            block, wide, starts,
            pl.BlockSpec((heads, width, 2 * width), lambda i: (0, 0, 0)),
        ],
        out_shape=[
            jax.ShapeDtypeStruct((rows, channel_count), BF16),
            jax.ShapeDtypeStruct((rows, 2 * channel_count), BF16),
            jax.ShapeDtypeStruct((steps, heads, width, 2 * width), BF16),
            jax.ShapeDtypeStruct((heads, width, 2 * width), BF16),
        ],
        scratch_shapes=[pltpu.VMEM((heads, width, 2 * width), F32)],
        compiler_params=params,
        name="summary",
    )(rim, key_raw, value_raw, key_raw, value_raw, log_decay, write_strength, conv_weight, masks)
    local, qeff = pl.pallas_call(
        local_kernel,
        grid=(steps,),
        in_specs=[rims, block, prev, block, wide, starts, gates, taps],
        out_specs=[block, block],
        out_shape=[
            jax.ShapeDtypeStruct((rows, channel_count), F32),
            jax.ShapeDtypeStruct((rows, channel_count), BF16),
        ],
        compiler_params=params,
        name="local",
    )(rim, query_raw, query_raw, keys, fresh, start, log_decay, conv_weight)
    return local, qeff, summary


def out_kernel(
    info_ref, state_ref, local_ref, qeff_ref, gate_ref, gain_ref, weight_ref, out_ref
):
    heads, width = state_ref.shape[0], state_ref.shape[1]
    rows = local_ref.shape[0]
    base = info_ref[0] + info_ref[1] * rows
    valid = base + lax.broadcasted_iota(jnp.int32, (rows, width), 0) < info_ref[2]
    gated = []
    for h in range(heads):
        sl = slice(h * width, (h + 1) * width)
        o = local_ref[:, sl] + mm(qeff_ref[:, sl], state_ref[h].astype(BF16))
        norm = lax.rsqrt(jnp.mean(o * o, axis=-1, keepdims=True) + 1e-06)
        g = gate_ref[:, sl].astype(F32)
        o = o * norm * gain_ref[...] * (g * sigmoid(g))
        gated.append(jnp.where(valid, o, 0.0).astype(BF16))
    out_ref[...] = mm(jnp.concatenate(gated, axis=1), weight_ref[...]).astype(BF16)


def passed_along(block, axis, distance):
    devices = range(lax.axis_size(axis))
    route = [(i - distance, i) for i in devices if i - distance in devices]
    return lax.ppermute(block, axis, route)


def carried_in(summary, axis):
    width = summary.shape[1]
    count = lax.axis_size(axis)
    move, own = summary[:, :, :width], summary[:, :, width:]

    def apply(a, b, s):
        return jnp.einsum("hij,hjk->hik", a, s, preferred_element_type=F32) + b.astype(F32)

    if count == 4:
        got = lax.ppermute(summary, axis, [(0, 1), (2, 3)])
        got_move, got_own = got[:, :, :width], got[:, :, width:]
        pair = apply(move, own, got_own).astype(BF16)
        near = lax.ppermute(pair, axis, [(1, 2)])
        far = lax.ppermute(pair, axis, [(1, 3)])
        return apply(got_move, got_own, far) + near.astype(F32)
    state = passed_along(own, axis, 1)
    for _ in range(count - 2):
        state = passed_along(apply(move, own, state).astype(BF16), axis, 1)
    return state.astype(F32)


def on_device(
    query_raw, key_raw, value_raw, out_gate, log_decay, write_strength,
    conv_weight, norm_gain, out_weight, history_end,
):
    rows, channel_count = query_raw.shape
    heads = log_decay.shape[0]
    width = channel_count // heads
    rim = passed_along(
        jnp.stack([query_raw[-RIM:], key_raw[-RIM:], value_raw[-RIM:]]), "seq", 1
    )
    local, qeff, summary = front(
        rim, query_raw, key_raw, value_raw, log_decay, write_strength, conv_weight
    )
    state = carried_in(summary, "seq")
    owners = lax.axis_size("head")
    mine = lax.axis_index("head")
    tile = rows // owners
    dim = out_weight.shape[1]
    start = lax.axis_index("seq") * rows
    gain = norm_gain.reshape(1, width)

    def partial(owner):
        info = jnp.stack([start, owner, history_end[0]]).astype(jnp.int32)
        tiles = pl.BlockSpec((tile, channel_count), lambda i, s: (s[1], 0))
        return pl.pallas_call(
            out_kernel,
            grid_spec=pltpu.PrefetchScalarGridSpec(
                num_scalar_prefetch=1,
                grid=(1,),
                in_specs=[
                    pl.BlockSpec((heads, width, width), lambda i, s: (0, 0, 0)),
                    tiles, tiles, tiles,
                    pl.BlockSpec((1, width), lambda i, s: (0, 0)),
                    pl.BlockSpec((channel_count, dim), lambda i, s: (0, 0)),
                ],
                out_specs=pl.BlockSpec((tile, dim), lambda i, s: (0, 0)),
            ),
            out_shape=jax.ShapeDtypeStruct((tile, dim), BF16),
            compiler_params=pltpu.CompilerParams(vmem_limit_bytes=48 << 20),
            name="outputs",
        )(info, state, local, qeff, out_gate, gain, out_weight)

    def exchange(block, bit):
        return lax.ppermute(block, "head", [(i, i ^ bit) for i in range(owners)])

    def added(a, b):
        return (a.astype(F32) + b.astype(F32)).astype(BF16)

    if owners != 4:
        blocks = jnp.concatenate([partial(o) for o in range(owners)], axis=0)
        return lax.psum_scatter(blocks, "head", scatter_dimension=0, tiled=True)
    far_in = exchange(partial(mine ^ 3), 1)
    far = added(partial(mine ^ 2), far_in)
    far_got = exchange(far, 2)
    near_in = exchange(partial(mine ^ 1), 1)
    near = partial(mine).astype(F32) + near_in.astype(F32)
    return (near + far_got.astype(F32)).astype(BF16)


def solution(mesh):
    return jax.shard_map(
        on_device,
        mesh=mesh,
        in_specs=(
            P(("parts", "seq"), "head"),
            P(("parts", "seq"), "head"),
            P(("parts", "seq"), "head"),
            P(("parts", "seq"), "head"),
            P("head", ("parts", "seq")),
            P("head", ("parts", "seq")),
            P(None, None, "head"),
            P(),
            P("head", None),
            P("parts"),
        ),
        out_specs=P(("parts", "seq", "head"), None),
        check_vma=False,
    )
```

```python
import functools

import jax
import jax.numpy as jnp
import numpy as np
from jax import lax
from jax.experimental import pallas as pl
from jax.experimental.pallas import tpu as pltpu
from jax.sharding import PartitionSpec as P

CHUNK = 128
RIM = 16
GROUP = 8
SUBS = 2
PIECES = 1
F32 = jnp.float32
BF16 = jnp.bfloat16
NN = (((1,), (0,)), ((), ()))
NT = (((1,), (1,)), ((), ()))


def mm(left, right, dims=NN):
    return lax.dot_general(left, right, dims, preferred_element_type=F32)


def exact(left, right, dims=NN):
    return lax.dot_general(
        left, right, dims, precision=lax.Precision.HIGHEST, preferred_element_type=F32
    )


def sigmoid(x):
    return 1.0 / (1.0 + jnp.exp(-x))


def conv_silu(raw, rim, taps):
    rows = raw.shape[0]
    padded = jnp.concatenate([rim, raw], axis=0)
    n = rim.shape[0]
    total = taps[3:4] * raw
    for j in range(3):
        total = total + taps[j : j + 1] * padded[n - 3 + j : n - 3 + j + rows]
    return total * sigmoid(total)


def unit(x, scale):
    return (x * (lax.rsqrt(jnp.sum(x * x, axis=-1, keepdims=True) + 1e-06) * scale)).astype(BF16)


def placed(*arrays):
    return [pltpu.with_memory_space_constraint(x, pltpu.HBM) for x in arrays]


def positions(c):
    return (
        lax.broadcasted_iota(jnp.int32, (c, c), 0),
        lax.broadcasted_iota(jnp.int32, (c, c), 1),
    )


def channels(rim_ref, ref, prev_ref, taps_ref, which, sl, first):
    raw = ref[:, sl].astype(F32)
    rim = jnp.where(first, rim_ref[which, :, sl].astype(F32), prev_ref[:, sl].astype(F32))
    return conv_silu(raw, rim[-8:], taps_ref[which, :, sl])


def summary_kernel(
    rim_ref, k_ref, v_ref, kp_ref, vp_ref, dec_ref, wr_ref, taps_ref, mask_ref,
    keys_ref, fresh_ref, start_ref, summary_ref, state_ref,
):
    step = pl.program_id(0)
    c = CHUNK
    subs = k_ref.shape[0] // c
    heads = dec_ref.shape[0]
    width = k_ref.shape[1] // heads

    @pl.when(step == 0)
    def _():
        rows = lax.broadcasted_iota(jnp.int32, (width, 2 * width), 0)
        cols = lax.broadcasted_iota(jnp.int32, (width, 2 * width), 1)
        eye = jnp.where(rows == cols, 1.0, 0.0).astype(F32)
        for h in range(heads):
            state_ref[h] = eye

    ri, ci = positions(c)
    tril = jnp.where(ci <= ri, 1.0, 0.0).astype(F32)
    eye = jnp.where(ci == ri, 1.0, 0.0).astype(F32)
    first = step == 0
    dec = [dec_ref[:, s * c : (s + 1) * c] for s in range(subs)]
    wr = [wr_ref[:, s * c : (s + 1) * c] for s in range(subs)]
    cum_row = [exact(x, tril, NT) for x in dec]
    cum_col = [exact(tril, x, NT) for x in dec]
    wr_col = [exact(eye, x, NT) for x in wr]
    last = [x[:, c - 1 : c] for x in cum_row]
    wg_row = [wr[s] * jnp.exp(cum_row[s]) for s in range(subs)]
    kout_row = [jnp.exp(last[s] - cum_row[s]) for s in range(subs)]
    last_decay = [jnp.exp(x) for x in last]

    units = [(s, h) for s in range(subs) for h in range(heads)]
    n = range(len(units))

    def lanes(h):
        return slice(h * width, (h + 1) * width)

    def row(x, i):
        s, h = units[i]
        return x[s][h : h + 1, :]

    def col(x, i):
        s, h = units[i]
        return x[s][:, h : h + 1]

    def split(x):
        return {(s, h): x[h][s * c : (s + 1) * c] for s, h in units}

    k_all = [unit(channels(rim_ref, k_ref, kp_ref, taps_ref, 1, lanes(h), first), 1.0) for h in range(heads)]
    for h in range(heads):
        keys_ref[:, lanes(h)] = k_all[h]
    k = [k_all[h][s * c : (s + 1) * c] for s, h in units]
    gram = [mm(x, x, NT) for x in k]
    low = []
    for i in n:
        gap = col(cum_col, i) - row(cum_row, i)
        decay = jnp.exp(jnp.minimum(gap, 0.0)) * col(wr_col, i)
        low.append(jnp.where(ci < ri, gram[i] * decay, 0.0).astype(BF16))
    inv = [eye - (x * mask_ref[0]).astype(F32) for x in low]
    level = 1
    while (1 << level) < c:
        mask = mask_ref[level]
        invb = [x.astype(BF16) for x in inv]
        inner = [mm(low[i] * mask, invb[i]).astype(BF16) for i in n]
        inv = [inv[i] - mm(invb[i], inner[i]) for i in n]
        level += 1
    v_all = [channels(rim_ref, v_ref, vp_ref, taps_ref, 2, lanes(h), first).astype(BF16) for h in range(heads)]
    v = [v_all[h][s * c : (s + 1) * c] for s, h in units]
    key_mix = [mm((inv[i] * row(wg_row, i)).astype(BF16), k[i]).astype(BF16) for i in n]
    value_mix = [mm((inv[i] * row(wr, i)).astype(BF16), v[i]) for i in n]
    k_out = [(k[i].astype(F32).T * row(kout_row, i)).astype(BF16) for i in n]
    for s in range(subs):
        at = s * heads
        start = [state_ref[h].astype(BF16) for h in range(heads)]
        for h in range(heads):
            start_ref[s, h] = start[h]
        read = [mm(key_mix[at + h], start[h]) for h in range(heads)]
        fresh = [
            jnp.concatenate(
                [-read[h][:, :width], value_mix[at + h] - read[h][:, width:]], axis=1
            ).astype(BF16)
            for h in range(heads)
        ]
        for h in range(heads):
            fresh_ref[s * c : (s + 1) * c, 2 * h * width : 2 * (h + 1) * width] = fresh[h]
        both = [mm(k_out[at + h], fresh[h]) for h in range(heads)]
        for h in range(heads):
            state_ref[h] = last_decay[s][h : h + 1, :] * state_ref[h] + both[h]

    @pl.when(step == pl.num_programs(0) - 1)
    def _():
        summary_ref[...] = state_ref[...].astype(BF16)


def local_kernel(
    begin, rim_ref, q_ref, qp_ref, keys_ref, fresh_ref, start_ref, dec_ref, taps_ref, *rest
):
    local_ref, qeff_ref = rest[-2:]
    step = pl.program_id(0) + begin
    c = q_ref.shape[0]
    heads = dec_ref.shape[0]
    width = q_ref.shape[1] // heads
    ri, ci = positions(c)
    tril = jnp.where(ci <= ri, 1.0, 0.0).astype(F32)
    dec = dec_ref[...]
    cum_row = exact(dec, tril, NT)
    cum_col = exact(tril, dec, NT)
    gamma_col = jnp.exp(cum_col)
    first = step == 0
    for g in range(0, heads, GROUP):
        hs = range(g, g + GROUP)
        sls = [slice(h * width, (h + 1) * width) for h in hs]
        n = range(GROUP)
        q = [unit(channels(rim_ref, q_ref, qp_ref, taps_ref, 0, sl, first), width ** -0.5) for sl in sls]
        gram = [mm(q[i], keys_ref[:, sls[i]], NT) for i in n]
        for i in n:
            h = hs[i]
            gap = cum_col[:, h : h + 1] - cum_row[h : h + 1, :]
            scores = jnp.where(ci <= ri, gram[i] * jnp.exp(jnp.minimum(gap, 0.0)), 0.0).astype(BF16)
            q_in = (q[i].astype(F32) * gamma_col[:, h : h + 1]).astype(BF16)
            out = mm(
                jnp.concatenate([q_in, scores], axis=1),
                jnp.concatenate(
                    [start_ref[0, h], fresh_ref[:, 2 * h * width : 2 * (h + 1) * width]], axis=0
                ),
            )
            qeff_ref[:, sls[i]] = out[:, :width].astype(BF16)
            local_ref[:, sls[i]] = out[:, width:]


def level_masks(c):
    r = np.arange(c)
    differ = r[:, None] ^ r[None, :]
    lower = r[:, None] > r[None, :]
    levels = []
    size = 1
    while size < c:
        levels.append(lower & (differ >= size) & (differ < 2 * size))
        size *= 2
    return jnp.asarray(np.stack(levels), BF16)


def front(rim, query_raw, key_raw, value_raw, log_decay, write_strength, conv_weight):
    rows, channel_count = query_raw.shape
    heads = log_decay.shape[0]
    width = channel_count // heads
    c = CHUNK
    steps = rows // c
    per = c // RIM
    masks = level_masks(c)
    block = pl.BlockSpec((c, channel_count), lambda i: (i, 0))
    wide = pl.BlockSpec((c, 2 * channel_count), lambda i: (i, 0))
    prev = pl.BlockSpec((RIM, channel_count), lambda i: (jnp.maximum(i * per - 1, 0), 0))
    gates = pl.BlockSpec((heads, c), lambda i: (0, i))
    rims = pl.BlockSpec((3, RIM, channel_count), lambda i: (0, 0, 0))
    taps = pl.BlockSpec((3, 4, channel_count), lambda i: (0, 0, 0))
    starts = pl.BlockSpec((1, heads, width, 2 * width), lambda i: (i, 0, 0, 0))
    params = pltpu.CompilerParams(vmem_limit_bytes=48 << 20)
    subs = SUBS if steps % SUBS == 0 else 1
    big = pl.BlockSpec((subs * c, channel_count), lambda i: (i, 0))
    keys, fresh, start, summary = pl.pallas_call(
        summary_kernel,
        grid=(steps // subs,),
        in_specs=[
            rims, big, big,
            pl.BlockSpec((RIM, channel_count), lambda i: (jnp.maximum(i * per * subs - 1, 0), 0)),
            pl.BlockSpec((RIM, channel_count), lambda i: (jnp.maximum(i * per * subs - 1, 0), 0)),
            pl.BlockSpec((heads, subs * c), lambda i: (0, i)),
            pl.BlockSpec((heads, subs * c), lambda i: (0, i)), taps,
            pl.BlockSpec(masks.shape, lambda i: (0, 0, 0)),
        ],
        out_specs=[
            big,
            pl.BlockSpec((subs * c, 2 * channel_count), lambda i: (i, 0)),
            pl.BlockSpec((subs, heads, width, 2 * width), lambda i: (i, 0, 0, 0)),
            pl.BlockSpec((heads, width, 2 * width), lambda i: (0, 0, 0)),
        ],
        out_shape=[
            pltpu.HBM((rows, channel_count), BF16),
            pltpu.HBM((rows, 2 * channel_count), BF16),
            pltpu.HBM((steps, heads, width, 2 * width), BF16),
            jax.ShapeDtypeStruct((heads, width, 2 * width), BF16),
        ],
        scratch_shapes=[pltpu.VMEM((heads, width, 2 * width), F32)],
        compiler_params=params,
        name="summary",
    )(rim, *placed(key_raw, value_raw, key_raw, value_raw, log_decay, write_strength, conv_weight, masks))
    first = steps // 2

    def local_part(begin, count, done, rim, keys, fresh, start):
        def at(spec):
            return pl.BlockSpec(spec.block_shape, lambda i: spec.index_map(i + begin))

        return pl.pallas_call(
            functools.partial(local_kernel, begin),
            grid=(count,),
            in_specs=[rims, *map(at, (block, prev, block, wide, starts, gates)), taps]
            + [pl.BlockSpec(memory_space=pl.ANY)] * len(done),
            out_specs=[at(block), at(block)],
            out_shape=[
                pltpu.HBM((rows, channel_count), F32),
                pltpu.HBM((rows, channel_count), BF16),
            ],
            input_output_aliases={8 + i: i for i in range(len(done))},
            compiler_params=params,
            name="local",
        )(rim, *placed(query_raw, query_raw, keys, fresh, start, log_decay, conv_weight, *done))

    def early():
        return local_part(0, first, (), rim, keys, fresh, start)

    def late(done):
        return local_part(first, steps - first, done, rim, keys, fresh, start)

    return early, late, summary


def out_kernel(
    info_ref, state_ref, local_ref, qeff_ref, gate_ref, gain_ref, weight_ref, out_ref
):
    heads, width = state_ref.shape[0], state_ref.shape[1]
    rows = local_ref.shape[0]
    base = info_ref[0] + info_ref[1] * rows
    valid = base + lax.broadcasted_iota(jnp.int32, (rows, width), 0) < info_ref[2]
    gated = []
    for h in range(heads):
        sl = slice(h * width, (h + 1) * width)
        o = local_ref[:, sl] + mm(qeff_ref[:, sl], state_ref[h].astype(BF16))
        norm = lax.rsqrt(jnp.mean(o * o, axis=-1, keepdims=True) + 1e-06)
        g = gate_ref[:, sl].astype(F32)
        o = o * norm * gain_ref[...] * (g * sigmoid(g))
        gated.append(jnp.where(valid, o, 0.0).astype(BF16))
    gated = jnp.concatenate(gated, axis=1)
    out_ref[...] = mm(gated, weight_ref[...]).astype(BF16)


def passed_along(block, axis, distance):
    devices = range(lax.axis_size(axis))
    route = [(i - distance, i) for i in devices if i - distance in devices]
    return lax.ppermute(block, axis, route)


def carried_in(summary, axis, early, late):
    width = summary.shape[1]
    count = lax.axis_size(axis)
    move, own = summary[:, :, :width], summary[:, :, width:]

    def apply(a, b, s):
        return jnp.einsum("hij,hjk->hik", a, s, preferred_element_type=F32) + b.astype(F32)

    if count == 4:
        got_own = lax.ppermute(own, axis, [(0, 1), (2, 3)])
        done = early()
        got_own, done = lax.optimization_barrier((got_own, done))
        pair = apply(move, own, got_own).astype(BF16)
        far = lax.ppermute(pair, axis, [(1, 3)])
        near = lax.ppermute(pair, axis, [(1, 2)])
        move, done, pair = lax.optimization_barrier((move, done, pair))
        got_move = lax.ppermute(move, axis, [(2, 3)])
        done = late(done)
        return apply(got_move, got_own, far) + near.astype(F32), *done
    state = passed_along(own, axis, 1)
    for _ in range(count - 2):
        state = passed_along(apply(move, own, state).astype(BF16), axis, 1)
    return state.astype(F32), *late(early())


def on_device(
    query_raw, key_raw, value_raw, out_gate, log_decay, write_strength,
    conv_weight, norm_gain, out_weight, history_end,
):
    rows, channel_count = query_raw.shape
    heads = log_decay.shape[0]
    width = channel_count // heads
    rim = passed_along(
        jnp.stack([query_raw[-RIM:], key_raw[-RIM:], value_raw[-RIM:]]), "seq", 1
    )
    early, late, summary = front(
        rim, query_raw, key_raw, value_raw, log_decay, write_strength, conv_weight
    )
    state, local, qeff = carried_in(summary, "seq", early, late)
    owners = lax.axis_size("head")
    mine = lax.axis_index("head")
    dim = out_weight.shape[1]
    start = lax.axis_index("seq") * rows
    gain = norm_gain.reshape(1, width)

    def partial(owner, piece=0, pieces=1, after=None, resident=False):
        tile = rows // owners // pieces
        info = jnp.stack([start, owner * pieces + piece, history_end[0]]).astype(jnp.int32)
        if after is not None:
            info, after = lax.optimization_barrier((info, after))
        tiles = pl.BlockSpec((tile, channel_count), lambda i, s: (s[1], 0))
        weight = out_weight if resident else placed(out_weight)[0]
        return pl.pallas_call(
            out_kernel,
            grid_spec=pltpu.PrefetchScalarGridSpec(
                num_scalar_prefetch=1,
                grid=(1,),
                in_specs=[
                    pl.BlockSpec((heads, width, width), lambda i, s: (0, 0, 0)),
                    tiles, tiles, tiles,
                    pl.BlockSpec((1, width), lambda i, s: (0, 0)),
                    pl.BlockSpec(memory_space=pltpu.VMEM)
                    if resident
                    else pl.BlockSpec((channel_count, dim), lambda i, s: (0, 0)),
                ],
                out_specs=pl.BlockSpec((tile, dim), lambda i, s: (0, 0)),
            ),
            out_shape=jax.ShapeDtypeStruct((tile, dim), BF16),
            compiler_params=pltpu.CompilerParams(vmem_limit_bytes=24 << 20),
            name="outputs",
        )(info, state, *placed(local, qeff, out_gate, gain), weight)

    def exchange(block, bit):
        return lax.ppermute(block, "head", [(i, i ^ bit) for i in range(owners)])

    def added(a, b):
        return (a.astype(F32) + b.astype(F32)).astype(BF16)

    if owners != 4:
        blocks = jnp.concatenate([partial(o) for o in range(owners)], axis=0)
        return lax.psum_scatter(blocks, "head", scatter_dimension=0, tiled=True)
    far, far_got = None, []
    for piece in range(PIECES):
        sent = partial(mine ^ 3, piece, PIECES, far, resident=piece == 0)
        far_in = exchange(sent, 1)
        far = added(partial(mine ^ 2, piece, PIECES, sent), far_in)
        far_got.append(exchange(far, 2))
    near_in = exchange(partial(mine ^ 1, after=far), 1)
    near = partial(mine, after=far).astype(F32) + near_in.astype(F32)
    tile = near.shape[0] // PIECES
    return jnp.concatenate(
        [
            (near[i * tile : (i + 1) * tile] + got.astype(F32)).astype(BF16)
            for i, got in enumerate(far_got)
        ],
        axis=0,
    )


def solution(mesh):
    return jax.shard_map(
        on_device,
        mesh=mesh,
        in_specs=(
            P(("parts", "seq"), "head"),
            P(("parts", "seq"), "head"),
            P(("parts", "seq"), "head"),
            P(("parts", "seq"), "head"),
            P("head", ("parts", "seq")),
            P("head", ("parts", "seq")),
            P(None, None, "head"),
            P(),
            P("head", None),
            P("parts"),
        ),
        out_specs=P(("parts", "seq", "head"), None),
        check_vma=False,
    )
```

```python
import functools

import jax
import jax.numpy as jnp
import numpy as np
from jax import lax
from jax.experimental import pallas as pl
from jax.experimental.pallas import tpu as pltpu
from jax.sharding import PartitionSpec as P

CHUNK = 128
RIM = 16
GROUP = 8
SUBS = 2
PIECES = 1
F32 = jnp.float32
BF16 = jnp.bfloat16
NN = (((1,), (0,)), ((), ()))
NT = (((1,), (1,)), ((), ()))


def mm(left, right, dims=NN):
    return lax.dot_general(left, right, dims, preferred_element_type=F32)


def exact(left, right, dims=NN):
    return lax.dot_general(
        left, right, dims, precision=lax.Precision.HIGHEST, preferred_element_type=F32
    )


def sigmoid(x):
    return 0.5 + 0.5 * jnp.tanh(0.5 * x)


def conv_silu(raw, rim, taps):
    rows, n = raw.shape[0], rim.shape[0]
    padded = jnp.concatenate([rim, raw], axis=0)
    before = pltpu.roll(padded, 1, 0)
    old = pltpu.roll(taps[1:2] * padded + taps[0:1] * before, 2, 0)
    total = (taps[3:4] * padded + taps[2:3] * before + old)[n:]
    return total * sigmoid(total)


def unit(x, scale):
    return (x * (lax.rsqrt(jnp.sum(x * x, axis=-1, keepdims=True) + 1e-06) * scale)).astype(BF16)


def placed(*arrays):
    return [pltpu.with_memory_space_constraint(x, pltpu.HBM) for x in arrays]


def positions(c):
    return (
        lax.broadcasted_iota(jnp.int32, (c, c), 0),
        lax.broadcasted_iota(jnp.int32, (c, c), 1),
    )


def channels(rim_ref, ref, prev_ref, taps_ref, which, sl, first):
    raw = ref[:, sl].astype(F32)
    rim = jnp.where(first, rim_ref[which, :, sl].astype(F32), prev_ref[:, sl].astype(F32))
    return conv_silu(raw, rim[-8:], taps_ref[which, :, sl])


def summary_kernel(
    rim_ref, k_ref, v_ref, kp_ref, vp_ref, dec_ref, wr_ref, taps_ref, mask_ref,
    keys_ref, fresh_ref, start_ref, summary_ref, state_ref,
):
    step = pl.program_id(0)
    c = CHUNK
    subs = k_ref.shape[0] // c
    heads = dec_ref.shape[0]
    width = k_ref.shape[1] // heads

    @pl.when(step == 0)
    def _():
        rows = lax.broadcasted_iota(jnp.int32, (width, 2 * width), 0)
        cols = lax.broadcasted_iota(jnp.int32, (width, 2 * width), 1)
        eye = jnp.where(rows == cols, 1.0, 0.0).astype(F32)
        for h in range(heads):
            state_ref[h] = eye

    ri, ci = positions(c)
    tril = jnp.where(ci <= ri, 1.0, 0.0).astype(F32)
    eye = jnp.where(ci == ri, 1.0, 0.0).astype(F32)
    first = step == 0
    dec = [dec_ref[:, s * c : (s + 1) * c] for s in range(subs)]
    wr = [wr_ref[:, s * c : (s + 1) * c] for s in range(subs)]
    cum_row = [exact(x, tril, NT) for x in dec]
    cum_col = [exact(tril, x, NT) for x in dec]
    wr_col = [exact(eye, x, NT) for x in wr]
    last = [x[:, c - 1 : c] for x in cum_row]
    log_col = [cum_col[s] + jnp.log(wr_col[s]) for s in range(subs)]
    drop_col = [-wr_col[s] * jnp.exp(cum_col[s]) for s in range(subs)]
    kout_row = [jnp.exp(last[s] - cum_row[s]) for s in range(subs)]
    last_decay = [jnp.exp(x) for x in last]

    units = [(s, h) for s in range(subs) for h in range(heads)]
    n = range(len(units))

    def lanes(h):
        return slice(h * width, (h + 1) * width)

    def row(x, i):
        s, h = units[i]
        return x[s][h : h + 1, :]

    def col(x, i):
        s, h = units[i]
        return x[s][:, h : h + 1]

    def split(x):
        return {(s, h): x[h][s * c : (s + 1) * c] for s, h in units}

    k_all = [unit(channels(rim_ref, k_ref, kp_ref, taps_ref, 1, lanes(h), first), 1.0) for h in range(heads)]
    for h in range(heads):
        keys_ref[:, lanes(h)] = k_all[h]
    k = [k_all[h][s * c : (s + 1) * c] for s, h in units]
    gram = [mm(x, x, NT) for x in k]
    low = []
    for i in n:
        decay = jnp.exp(col(log_col, i) - row(cum_row, i))
        low.append(jnp.where(ci < ri, gram[i] * decay, 0.0).astype(BF16))
    inv = [eye.astype(BF16) - x * mask_ref[0] for x in low]
    level = 1
    while (1 << level) < c:
        mask = mask_ref[level]
        inner = [mm(low[i] * mask, inv[i]).astype(BF16) for i in n]
        inv = [inv[i] - mm(inv[i], inner[i]).astype(BF16) for i in n]
        level += 1
    v_all = [channels(rim_ref, v_ref, vp_ref, taps_ref, 2, lanes(h), first).astype(BF16) for h in range(heads)]
    v = [v_all[h][s * c : (s + 1) * c] for s, h in units]
    kf = [x.astype(F32) for x in k]
    sides = [
        jnp.concatenate(
            [
                (kf[i] * col(drop_col, i)).astype(BF16),
                (v[i].astype(F32) * col(wr_col, i)).astype(BF16),
            ],
            axis=1,
        )
        for i in n
    ]
    mixed = [mm(inv[i], sides[i]) for i in n]
    k_out = [(kf[i].T * row(kout_row, i)).astype(BF16) for i in n]
    for s in range(subs):
        at = s * heads
        start = [state_ref[h].astype(BF16) for h in range(heads)]
        for h in range(heads):
            start_ref[s, h] = start[h]
        read = [mm(mixed[at + h][:, :width].astype(BF16), start[h]) for h in range(heads)]
        fresh = [
            jnp.concatenate(
                [read[h][:, :width], mixed[at + h][:, width:] + read[h][:, width:]], axis=1
            ).astype(BF16)
            for h in range(heads)
        ]
        for h in range(heads):
            fresh_ref[s * c : (s + 1) * c, 2 * h * width : 2 * (h + 1) * width] = fresh[h]
        both = [mm(k_out[at + h], fresh[h]) for h in range(heads)]
        for h in range(heads):
            state_ref[h] = last_decay[s][h : h + 1, :] * state_ref[h] + both[h]

    @pl.when(step == pl.num_programs(0) - 1)
    def _():
        summary_ref[...] = state_ref[...].astype(BF16)


def local_kernel(
    begin, rim_ref, q_ref, qp_ref, keys_ref, fresh_ref, start_ref, dec_ref, taps_ref, *rest
):
    local_ref, qeff_ref = rest[-2:]
    step = pl.program_id(0) + begin
    c = q_ref.shape[0]
    heads = dec_ref.shape[0]
    width = q_ref.shape[1] // heads
    ri, ci = positions(c)
    tril = jnp.where(ci <= ri, 1.0, 0.0).astype(F32)
    dec = dec_ref[...]
    cum_row = exact(dec, tril, NT)
    cum_col = exact(tril, dec, NT)
    gamma_col = jnp.exp(cum_col)
    first = step == 0
    for g in range(0, heads, GROUP):
        hs = range(g, g + GROUP)
        sls = [slice(h * width, (h + 1) * width) for h in hs]
        n = range(GROUP)
        q = [unit(channels(rim_ref, q_ref, qp_ref, taps_ref, 0, sl, first), width ** -0.5) for sl in sls]
        gram = [mm(q[i], keys_ref[:, sls[i]], NT) for i in n]
        for i in n:
            h = hs[i]
            gap = cum_col[:, h : h + 1] - cum_row[h : h + 1, :]
            scores = jnp.where(ci <= ri, gram[i] * jnp.exp(gap), 0.0).astype(BF16)
            q_in = (q[i].astype(F32) * gamma_col[:, h : h + 1]).astype(BF16)
            out = mm(
                jnp.concatenate([q_in, scores], axis=1),
                jnp.concatenate(
                    [start_ref[0, h], fresh_ref[:, 2 * h * width : 2 * (h + 1) * width]], axis=0
                ),
            )
            qeff_ref[:, sls[i]] = out[:, :width].astype(BF16)
            local_ref[:, sls[i]] = out[:, width:]


def level_masks(c):
    r = np.arange(c)
    differ = r[:, None] ^ r[None, :]
    lower = r[:, None] > r[None, :]
    levels = []
    size = 1
    while size < c:
        levels.append(lower & (differ >= size) & (differ < 2 * size))
        size *= 2
    return jnp.asarray(np.stack(levels), BF16)


def front(rim, query_raw, key_raw, value_raw, log_decay, write_strength, conv_weight):
    rows, channel_count = query_raw.shape
    heads = log_decay.shape[0]
    width = channel_count // heads
    c = CHUNK
    steps = rows // c
    per = c // RIM
    masks = level_masks(c)
    block = pl.BlockSpec((c, channel_count), lambda i: (i, 0))
    wide = pl.BlockSpec((c, 2 * channel_count), lambda i: (i, 0))
    prev = pl.BlockSpec((RIM, channel_count), lambda i: (jnp.maximum(i * per - 1, 0), 0))
    gates = pl.BlockSpec((heads, c), lambda i: (0, i))
    rims = pl.BlockSpec((3, RIM, channel_count), lambda i: (0, 0, 0))
    taps = pl.BlockSpec((3, 4, channel_count), lambda i: (0, 0, 0))
    starts = pl.BlockSpec((1, heads, width, 2 * width), lambda i: (i, 0, 0, 0))
    params = pltpu.CompilerParams(vmem_limit_bytes=48 << 20)
    subs = SUBS if steps % SUBS == 0 else 1
    big = pl.BlockSpec((subs * c, channel_count), lambda i: (i, 0))
    keys, fresh, start, summary = pl.pallas_call(
        summary_kernel,
        grid=(steps // subs,),
        in_specs=[
            rims, big, big,
            pl.BlockSpec((RIM, channel_count), lambda i: (jnp.maximum(i * per * subs - 1, 0), 0)),
            pl.BlockSpec((RIM, channel_count), lambda i: (jnp.maximum(i * per * subs - 1, 0), 0)),
            pl.BlockSpec((heads, subs * c), lambda i: (0, i)),
            pl.BlockSpec((heads, subs * c), lambda i: (0, i)), taps,
            pl.BlockSpec(masks.shape, lambda i: (0, 0, 0)),
        ],
        out_specs=[
            big,
            pl.BlockSpec((subs * c, 2 * channel_count), lambda i: (i, 0)),
            pl.BlockSpec((subs, heads, width, 2 * width), lambda i: (i, 0, 0, 0)),
            pl.BlockSpec((heads, width, 2 * width), lambda i: (0, 0, 0)),
        ],
        out_shape=[
            pltpu.HBM((rows, channel_count), BF16),
            pltpu.HBM((rows, 2 * channel_count), BF16),
            pltpu.HBM((steps, heads, width, 2 * width), BF16),
            jax.ShapeDtypeStruct((heads, width, 2 * width), BF16),
        ],
        scratch_shapes=[pltpu.VMEM((heads, width, 2 * width), F32)],
        compiler_params=params,
        name="summary",
    )(rim, *placed(key_raw, value_raw, key_raw, value_raw, log_decay, write_strength, conv_weight, masks))
    first = steps // 3

    def local_part(begin, count, done, rim, keys, fresh, start):
        def at(spec):
            return pl.BlockSpec(spec.block_shape, lambda i: spec.index_map(i + begin))

        return pl.pallas_call(
            functools.partial(local_kernel, begin),
            grid=(count,),
            in_specs=[rims, *map(at, (block, prev, block, wide, starts, gates)), taps]
            + [pl.BlockSpec(memory_space=pl.ANY)] * len(done),
            out_specs=[at(block), at(block)],
            out_shape=[
                pltpu.HBM((rows, channel_count), F32),
                pltpu.HBM((rows, channel_count), BF16),
            ],
            input_output_aliases={8 + i: i for i in range(len(done))},
            compiler_params=params,
            name="local",
        )(rim, *placed(query_raw, query_raw, keys, fresh, start, log_decay, conv_weight, *done))

    def early():
        return local_part(0, first, (), rim, keys, fresh, start)

    def late(done):
        return local_part(first, steps - first, done, rim, keys, fresh, start)

    return early, late, summary


def out_kernel(
    info_ref, state_ref, local_ref, qeff_ref, gate_ref, gain_ref, weight_ref, out_ref
):
    heads, width = state_ref.shape[0], state_ref.shape[1]
    rows = local_ref.shape[0]
    base = info_ref[0] + info_ref[1] * rows
    valid = base + lax.broadcasted_iota(jnp.int32, (rows, width), 0) < info_ref[2]
    gated = []
    for h in range(heads):
        sl = slice(h * width, (h + 1) * width)
        o = local_ref[:, sl] + mm(qeff_ref[:, sl], state_ref[h].astype(BF16))
        norm = lax.rsqrt(jnp.mean(o * o, axis=-1, keepdims=True) + 1e-06)
        g = gate_ref[:, sl].astype(F32)
        o = o * norm * gain_ref[...] * (g * sigmoid(g))
        gated.append(jnp.where(valid, o, 0.0).astype(BF16))
    gated = jnp.concatenate(gated, axis=1)
    out_ref[...] = mm(gated, weight_ref[...]).astype(BF16)


def passed_along(block, axis, distance):
    devices = range(lax.axis_size(axis))
    route = [(i - distance, i) for i in devices if i - distance in devices]
    return lax.ppermute(block, axis, route)


def carried_in(summary, axis, early, late):
    width = summary.shape[1]
    count = lax.axis_size(axis)
    move, own = summary[:, :, :width], summary[:, :, width:]

    def apply(a, b, s):
        return jnp.einsum("hij,hjk->hik", a, s, preferred_element_type=F32) + b.astype(F32)

    if count == 4:
        got_own = lax.ppermute(own, axis, [(0, 1), (2, 3)])
        done = early()
        got_own, done = lax.optimization_barrier((got_own, done))
        pair = apply(move, own, got_own).astype(BF16)
        far = lax.ppermute(pair, axis, [(1, 3)])
        place = lax.axis_index(axis)
        next_in = lax.ppermute(jnp.where(place == 1, pair, move), axis, [(1, 2), (2, 3)])
        done, pair = lax.optimization_barrier((done, pair))
        done = late(done)
        got_move = jnp.where(place == 3, next_in, jnp.zeros_like(next_in))
        near = jnp.where(place == 2, next_in.astype(F32), 0.0)
        return apply(got_move, got_own, far) + near, *done
    state = passed_along(own, axis, 1)
    for _ in range(count - 2):
        state = passed_along(apply(move, own, state).astype(BF16), axis, 1)
    return state.astype(F32), *late(early())


def on_device(
    query_raw, key_raw, value_raw, out_gate, log_decay, write_strength,
    conv_weight, norm_gain, out_weight, history_end,
):
    rows, channel_count = query_raw.shape
    heads = log_decay.shape[0]
    width = channel_count // heads
    rim = passed_along(
        jnp.stack([query_raw[-RIM:], key_raw[-RIM:], value_raw[-RIM:]]), "seq", 1
    )
    early, late, summary = front(
        rim, query_raw, key_raw, value_raw, log_decay, write_strength, conv_weight
    )
    state, local, qeff = carried_in(summary, "seq", early, late)
    owners = lax.axis_size("head")
    mine = lax.axis_index("head")
    dim = out_weight.shape[1]
    start = lax.axis_index("seq") * rows
    gain = norm_gain.reshape(1, width)

    def partial(owner, piece=0, pieces=1, after=None, resident=False):
        tile = rows // owners // pieces
        info = jnp.stack([start, owner * pieces + piece, history_end[0]]).astype(jnp.int32)
        if after is not None:
            info, after = lax.optimization_barrier((info, after))
        tiles = pl.BlockSpec((tile, channel_count), lambda i, s: (s[1], 0))
        weight = out_weight if resident else placed(out_weight)[0]
        return pl.pallas_call(
            out_kernel,
            grid_spec=pltpu.PrefetchScalarGridSpec(
                num_scalar_prefetch=1,
                grid=(1,),
                in_specs=[
                    pl.BlockSpec((heads, width, width), lambda i, s: (0, 0, 0)),
                    tiles, tiles, tiles,
                    pl.BlockSpec((1, width), lambda i, s: (0, 0)),
                    pl.BlockSpec(memory_space=pltpu.VMEM)
                    if resident
                    else pl.BlockSpec((channel_count, dim), lambda i, s: (0, 0)),
                ],
                out_specs=pl.BlockSpec((tile, dim), lambda i, s: (0, 0)),
            ),
            out_shape=jax.ShapeDtypeStruct((tile, dim), BF16),
            compiler_params=pltpu.CompilerParams(vmem_limit_bytes=24 << 20),
            name="outputs",
        )(info, state, *placed(local, qeff, out_gate, gain), weight)

    def exchange(block, bit):
        return lax.ppermute(block, "head", [(i, i ^ bit) for i in range(owners)])

    def added(a, b):
        return (a.astype(F32) + b.astype(F32)).astype(BF16)

    if owners != 4:
        blocks = jnp.concatenate([partial(o) for o in range(owners)], axis=0)
        return lax.psum_scatter(blocks, "head", scatter_dimension=0, tiled=True)
    far, far_got = None, []
    for piece in range(PIECES):
        sent = partial(mine ^ 3, piece, PIECES, far, resident=piece == 0)
        far_in = exchange(sent, 1)
        far = added(partial(mine ^ 2, piece, PIECES, sent), far_in)
        far_got.append(exchange(far, 2))
    near_in = exchange(partial(mine ^ 1, after=far), 1)
    near = partial(mine, after=far).astype(F32) + near_in.astype(F32)
    tile = near.shape[0] // PIECES
    return jnp.concatenate(
        [
            (near[i * tile : (i + 1) * tile] + got.astype(F32)).astype(BF16)
            for i, got in enumerate(far_got)
        ],
        axis=0,
    )


def solution(mesh):
    return jax.shard_map(
        on_device,
        mesh=mesh,
        in_specs=(
            P(("parts", "seq"), "head"),
            P(("parts", "seq"), "head"),
            P(("parts", "seq"), "head"),
            P(("parts", "seq"), "head"),
            P("head", ("parts", "seq")),
            P("head", ("parts", "seq")),
            P(None, None, "head"),
            P(),
            P("head", None),
            P("parts"),
        ),
        out_specs=P(("parts", "seq", "head"), None),
        check_vma=False,
    )
```

```python
import functools

import jax
import jax.numpy as jnp
import numpy as np
from jax import lax
from jax.experimental import pallas as pl
from jax.experimental.pallas import tpu as pltpu
from jax.sharding import PartitionSpec as P

CHUNK = 128
RIM = 16
GROUP = 8
SUBS = 2
F32 = jnp.float32
BF16 = jnp.bfloat16
NN = (((1,), (0,)), ((), ()))
NT = (((1,), (1,)), ((), ()))


def mm(left, right, dims=NN):
    return lax.dot_general(left, right, dims, preferred_element_type=F32)


def exact(left, right, dims=NN):
    return lax.dot_general(
        left, right, dims, precision=lax.Precision.HIGHEST, preferred_element_type=F32
    )


def sigmoid(x):
    return 0.5 + 0.5 * jnp.tanh(0.5 * x)


def conv_silu(raw, rim, taps):
    rows, n = raw.shape[0], rim.shape[0]
    padded = jnp.concatenate([rim, raw], axis=0)
    before = pltpu.roll(padded, 1, 0)
    old = pltpu.roll(taps[1:2] * padded + taps[0:1] * before, 2, 0)
    total = (taps[3:4] * padded + taps[2:3] * before + old)[n:]
    return total * sigmoid(total)


def unit(x, scale):
    return (x * (lax.rsqrt(jnp.sum(x * x, axis=-1, keepdims=True) + 1e-06) * scale)).astype(BF16)


def placed(*arrays):
    return [pltpu.with_memory_space_constraint(x, pltpu.HBM) for x in arrays]


def positions(c):
    return (
        lax.broadcasted_iota(jnp.int32, (c, c), 0),
        lax.broadcasted_iota(jnp.int32, (c, c), 1),
    )


def channels(rim_ref, ref, prev_ref, taps_ref, which, sl, first):
    raw = ref[:, sl].astype(F32)
    rim = jnp.where(first, rim_ref[which, :, sl].astype(F32), prev_ref[:, sl].astype(F32))
    return conv_silu(raw, rim[-8:], taps_ref[which, :, sl])


def summary_kernel(
    rim_ref, k_ref, v_ref, kp_ref, vp_ref, dec_ref, wr_ref, taps_ref, mask_ref,
    keys_ref, fresh_ref, start_ref, summary_ref, state_ref,
):
    step = pl.program_id(0)
    c = CHUNK
    subs = k_ref.shape[0] // c
    heads = dec_ref.shape[0]
    width = k_ref.shape[1] // heads

    @pl.when(step == 0)
    def _():
        rows = lax.broadcasted_iota(jnp.int32, (width, 2 * width), 0)
        cols = lax.broadcasted_iota(jnp.int32, (width, 2 * width), 1)
        eye = jnp.where(rows == cols, 1.0, 0.0).astype(F32)
        for h in range(heads):
            state_ref[h] = eye

    ri, ci = positions(c)
    tril = jnp.where(ci <= ri, 1.0, 0.0).astype(F32)
    eye = jnp.where(ci == ri, 1.0, 0.0).astype(F32)
    first = step == 0
    dec = [dec_ref[:, s * c : (s + 1) * c] for s in range(subs)]
    wr = [wr_ref[:, s * c : (s + 1) * c] for s in range(subs)]
    cum_row = [exact(x, tril, NT) for x in dec]
    cum_col = [exact(tril, x, NT) for x in dec]
    wr_col = [exact(eye, x, NT) for x in wr]
    last = [x[:, c - 1 : c] for x in cum_row]
    log_col = [cum_col[s] + jnp.log(wr_col[s]) for s in range(subs)]
    drop_col = [-wr_col[s] * jnp.exp(cum_col[s]) for s in range(subs)]
    kout_row = [jnp.exp(last[s] - cum_row[s]) for s in range(subs)]
    last_decay = [jnp.exp(x) for x in last]

    units = [(s, h) for s in range(subs) for h in range(heads)]
    n = range(len(units))

    def lanes(h):
        return slice(h * width, (h + 1) * width)

    def row(x, i):
        s, h = units[i]
        return x[s][h : h + 1, :]

    def col(x, i):
        s, h = units[i]
        return x[s][:, h : h + 1]

    def split(x):
        return {(s, h): x[h][s * c : (s + 1) * c] for s, h in units}

    k_all = [unit(channels(rim_ref, k_ref, kp_ref, taps_ref, 1, lanes(h), first), 1.0) for h in range(heads)]
    for h in range(heads):
        keys_ref[:, lanes(h)] = k_all[h]
    k = [k_all[h][s * c : (s + 1) * c] for s, h in units]
    gram = [mm(x, x, NT) for x in k]
    low = []
    for i in n:
        decay = jnp.exp(col(log_col, i) - row(cum_row, i))
        low.append(jnp.where(ci < ri, gram[i] * decay, 0.0).astype(BF16))
    inv = [eye.astype(BF16) - x * mask_ref[0] for x in low]
    level = 1
    while (1 << level) < c:
        mask = mask_ref[level]
        inner = [mm(low[i] * mask, inv[i]).astype(BF16) for i in n]
        inv = [inv[i] - mm(inv[i], inner[i]).astype(BF16) for i in n]
        level += 1
    v_all = [channels(rim_ref, v_ref, vp_ref, taps_ref, 2, lanes(h), first).astype(BF16) for h in range(heads)]
    v = [v_all[h][s * c : (s + 1) * c] for s, h in units]
    kf = [x.astype(F32) for x in k]
    sides = [
        jnp.concatenate(
            [
                (kf[i] * col(drop_col, i)).astype(BF16),
                (v[i].astype(F32) * col(wr_col, i)).astype(BF16),
            ],
            axis=1,
        )
        for i in n
    ]
    mixed = [mm(inv[i], sides[i]) for i in n]
    k_out = [(kf[i].T * row(kout_row, i)).astype(BF16) for i in n]
    for s in range(subs):
        at = s * heads
        start = [state_ref[h].astype(BF16) for h in range(heads)]
        for h in range(heads):
            start_ref[s, h] = start[h]
        read = [mm(mixed[at + h][:, :width].astype(BF16), start[h]) for h in range(heads)]
        fresh = [
            jnp.concatenate(
                [read[h][:, :width], mixed[at + h][:, width:] + read[h][:, width:]], axis=1
            ).astype(BF16)
            for h in range(heads)
        ]
        for h in range(heads):
            fresh_ref[s * c : (s + 1) * c, 2 * h * width : 2 * (h + 1) * width] = fresh[h]
        both = [mm(k_out[at + h], fresh[h]) for h in range(heads)]
        for h in range(heads):
            state_ref[h] = last_decay[s][h : h + 1, :] * state_ref[h] + both[h]

    @pl.when(step == pl.num_programs(0) - 1)
    def _():
        summary_ref[...] = state_ref[...].astype(BF16)


def local_kernel(
    begin, rim_ref, q_ref, qp_ref, keys_ref, fresh_ref, start_ref, dec_ref, taps_ref, *rest
):
    local_ref, qeff_ref = rest[-2:]
    step = pl.program_id(0) + begin
    c = q_ref.shape[0]
    heads = dec_ref.shape[0]
    width = q_ref.shape[1] // heads
    ri, ci = positions(c)
    tril = jnp.where(ci <= ri, 1.0, 0.0).astype(F32)
    dec = dec_ref[...]
    cum_row = exact(dec, tril, NT)
    cum_col = exact(tril, dec, NT)
    gamma_col = jnp.exp(cum_col)
    first = step == 0
    for g in range(0, heads, GROUP):
        hs = range(g, g + GROUP)
        sls = [slice(h * width, (h + 1) * width) for h in hs]
        n = range(GROUP)
        q = [unit(channels(rim_ref, q_ref, qp_ref, taps_ref, 0, sl, first), width ** -0.5) for sl in sls]
        gram = [mm(q[i], keys_ref[:, sls[i]], NT) for i in n]
        for i in n:
            h = hs[i]
            gap = cum_col[:, h : h + 1] - cum_row[h : h + 1, :]
            scores = jnp.where(ci <= ri, gram[i] * jnp.exp(gap), 0.0).astype(BF16)
            q_in = (q[i].astype(F32) * gamma_col[:, h : h + 1]).astype(BF16)
            out = mm(
                jnp.concatenate([q_in, scores], axis=1),
                jnp.concatenate(
                    [start_ref[0, h], fresh_ref[:, 2 * h * width : 2 * (h + 1) * width]], axis=0
                ),
            )
            qeff_ref[:, sls[i]] = out[:, :width].astype(BF16)
            local_ref[:, sls[i]] = out[:, width:].astype(BF16)


def level_masks(c):
    r = np.arange(c)
    differ = r[:, None] ^ r[None, :]
    lower = r[:, None] > r[None, :]
    levels = []
    size = 1
    while size < c:
        levels.append(lower & (differ >= size) & (differ < 2 * size))
        size *= 2
    return jnp.asarray(np.stack(levels), BF16)


def front(rim, query_raw, key_raw, value_raw, log_decay, write_strength, conv_weight):
    rows, channel_count = query_raw.shape
    heads = log_decay.shape[0]
    width = channel_count // heads
    c = CHUNK
    steps = rows // c
    per = c // RIM
    masks = level_masks(c)
    block = pl.BlockSpec((c, channel_count), lambda i: (i, 0))
    wide = pl.BlockSpec((c, 2 * channel_count), lambda i: (i, 0))
    prev = pl.BlockSpec((RIM, channel_count), lambda i: (jnp.maximum(i * per - 1, 0), 0))
    gates = pl.BlockSpec((heads, c), lambda i: (0, i))
    rims = pl.BlockSpec((3, RIM, channel_count), lambda i: (0, 0, 0))
    taps = pl.BlockSpec((3, 4, channel_count), lambda i: (0, 0, 0))
    starts = pl.BlockSpec((1, heads, width, 2 * width), lambda i: (i, 0, 0, 0))
    params = pltpu.CompilerParams(vmem_limit_bytes=48 << 20)
    subs = SUBS if steps % SUBS == 0 else 1
    big = pl.BlockSpec((subs * c, channel_count), lambda i: (i, 0))
    keys, fresh, start, summary = pl.pallas_call(
        summary_kernel,
        grid=(steps // subs,),
        in_specs=[
            rims, big, big,
            pl.BlockSpec((RIM, channel_count), lambda i: (jnp.maximum(i * per * subs - 1, 0), 0)),
            pl.BlockSpec((RIM, channel_count), lambda i: (jnp.maximum(i * per * subs - 1, 0), 0)),
            pl.BlockSpec((heads, subs * c), lambda i: (0, i)),
            pl.BlockSpec((heads, subs * c), lambda i: (0, i)), taps,
            pl.BlockSpec(masks.shape, lambda i: (0, 0, 0)),
        ],
        out_specs=[
            big,
            pl.BlockSpec((subs * c, 2 * channel_count), lambda i: (i, 0)),
            pl.BlockSpec((subs, heads, width, 2 * width), lambda i: (i, 0, 0, 0)),
            pl.BlockSpec((heads, width, 2 * width), lambda i: (0, 0, 0)),
        ],
        out_shape=[
            pltpu.HBM((rows, channel_count), BF16),
            pltpu.HBM((rows, 2 * channel_count), BF16),
            pltpu.HBM((steps, heads, width, 2 * width), BF16),
            jax.ShapeDtypeStruct((heads, width, 2 * width), BF16),
        ],
        scratch_shapes=[pltpu.VMEM((heads, width, 2 * width), F32)],
        compiler_params=params,
        name="summary",
    )(rim, *placed(key_raw, value_raw, key_raw, value_raw, log_decay, write_strength, conv_weight, masks))
    first = steps // 3

    def local_part(begin, count, done, rim, keys, fresh, start):
        def at(spec):
            return pl.BlockSpec(spec.block_shape, lambda i: spec.index_map(i + begin))

        return pl.pallas_call(
            functools.partial(local_kernel, begin),
            grid=(count,),
            in_specs=[rims, *map(at, (block, prev, block, wide, starts, gates)), taps]
            + [pl.BlockSpec(memory_space=pl.ANY)] * len(done),
            out_specs=[at(block), at(block)],
            out_shape=[
                pltpu.HBM((rows, channel_count), BF16),
                pltpu.HBM((rows, channel_count), BF16),
            ],
            input_output_aliases={8 + i: i for i in range(len(done))},
            compiler_params=params,
            name="local",
        )(rim, *placed(query_raw, query_raw, keys, fresh, start, log_decay, conv_weight, *done))

    def early():
        return local_part(0, first, (), rim, keys, fresh, start)

    def late(done):
        return local_part(first, steps - first, done, rim, keys, fresh, start)

    return early, late, summary


def out_kernel(
    info_ref, state_ref, local_ref, qeff_ref, gate_ref, gain_ref, weight_ref, *out_refs
):
    step = pl.program_id(0)
    heads, width = state_ref.shape[0], state_ref.shape[1]
    rows = local_ref.shape[0]
    base = info_ref[0] + info_ref[2 + step] * rows
    valid = base + lax.broadcasted_iota(jnp.int32, (rows, width), 0) < info_ref[1]
    gated = []
    for h in range(heads):
        sl = slice(h * width, (h + 1) * width)
        o = local_ref[:, sl].astype(F32) + mm(qeff_ref[:, sl], state_ref[h])
        norm = lax.rsqrt(jnp.mean(o * o, axis=-1, keepdims=True) + 1e-06)
        g = gate_ref[:, sl].astype(F32)
        o = o * norm * gain_ref[...] * (g * sigmoid(g))
        gated.append(jnp.where(valid, o, 0.0).astype(BF16))
    result = mm(jnp.concatenate(gated, axis=1), weight_ref[...]).astype(BF16)
    for i, out_ref in enumerate(out_refs):

        @pl.when(step == i)
        def _(out_ref=out_ref):
            out_ref[...] = result


def passed_along(block, axis, distance):
    devices = range(lax.axis_size(axis))
    route = [(i - distance, i) for i in devices if i - distance in devices]
    return lax.ppermute(block, axis, route)


def ends_kernel(q_ref, k_ref, v_ref, out_ref):
    out_ref[0] = q_ref[...]
    out_ref[1] = k_ref[...]
    out_ref[2] = v_ref[...]


def ends(*arrays):
    rows, channel_count = arrays[0].shape
    last = rows // RIM - 1
    return pl.pallas_call(
        ends_kernel,
        grid=(1,),
        in_specs=[pl.BlockSpec((RIM, channel_count), lambda i: (last, 0))] * 3,
        out_specs=pl.BlockSpec((3, RIM, channel_count), lambda i: (0, 0, 0)),
        out_shape=jax.ShapeDtypeStruct((3, RIM, channel_count), BF16),
        name="ends",
    )(*placed(*arrays))


def carried_in(summary, axis, early, late):
    width = summary.shape[1]
    count = lax.axis_size(axis)
    move, own = summary[:, :, :width], summary[:, :, width:]

    def apply(a, b, s):
        return jnp.einsum("hij,hjk->hik", a, s, preferred_element_type=F32) + b.astype(F32)

    if count == 4:
        got_own = lax.ppermute(own, axis, [(0, 1), (2, 3)])
        done = early()
        got_own, done = lax.optimization_barrier((got_own, done))
        pair = apply(move, own, got_own).astype(BF16)
        far = lax.ppermute(pair, axis, [(1, 3)])
        place = lax.axis_index(axis)
        next_in = lax.ppermute(jnp.where(place == 1, pair, move), axis, [(1, 2), (2, 3)])
        done, pair = lax.optimization_barrier((done, pair))
        done = late(done)
        got_move = jnp.where(place == 3, next_in, jnp.zeros_like(next_in))
        near = jnp.where(place == 2, next_in.astype(F32), 0.0)
        return (apply(got_move, got_own, far) + near).astype(BF16), *done
    state = passed_along(own, axis, 1)
    for _ in range(count - 2):
        state = passed_along(apply(move, own, state).astype(BF16), axis, 1)
    return state, *late(early())


def on_device(
    query_raw, key_raw, value_raw, out_gate, log_decay, write_strength,
    conv_weight, norm_gain, out_weight, history_end,
):
    rows, channel_count = query_raw.shape
    heads = log_decay.shape[0]
    width = channel_count // heads
    rim = passed_along(ends(query_raw, key_raw, value_raw), "seq", 1)
    early, late, summary = front(
        rim, query_raw, key_raw, value_raw, log_decay, write_strength, conv_weight
    )
    state, local, qeff = carried_in(summary, "seq", early, late)
    owners = lax.axis_size("head")
    mine = lax.axis_index("head")
    dim = out_weight.shape[1]
    start = lax.axis_index("seq") * rows
    gain = norm_gain.reshape(1, width)

    def partial(*blocks, after=None, resident=False):
        tile = rows // owners
        info = jnp.stack([start, history_end[0], *blocks]).astype(jnp.int32)
        if after is not None:
            info, after = lax.optimization_barrier((info, after))
        tiles = pl.BlockSpec((tile, channel_count), lambda i, s: (s[2 + i], 0))
        weight = out_weight if resident else placed(out_weight)[0]
        return pl.pallas_call(
            out_kernel,
            grid_spec=pltpu.PrefetchScalarGridSpec(
                num_scalar_prefetch=1,
                grid=(len(blocks),),
                in_specs=[
                    pl.BlockSpec((heads, width, width), lambda i, s: (0, 0, 0)),
                    tiles, tiles, tiles,
                    pl.BlockSpec((1, width), lambda i, s: (0, 0)),
                    pl.BlockSpec(memory_space=pltpu.VMEM)
                    if resident
                    else pl.BlockSpec((channel_count, dim), lambda i, s: (0, 0)),
                ],
                out_specs=[pl.BlockSpec((tile, dim), lambda i, s: (0, 0))] * len(blocks),
            ),
            out_shape=[jax.ShapeDtypeStruct((tile, dim), BF16)] * len(blocks),
            compiler_params=pltpu.CompilerParams(vmem_limit_bytes=24 << 20),
            name="outputs",
        )(info, state, *placed(local, qeff, out_gate, gain), weight)

    def exchange(block, bit):
        return lax.ppermute(block, "head", [(i, i ^ bit) for i in range(owners)])

    def added(a, b):
        return (a.astype(F32) + b.astype(F32)).astype(BF16)

    if owners != 4:
        blocks = jnp.concatenate(partial(*range(owners)), axis=0)
        return lax.psum_scatter(blocks, "head", scatter_dimension=0, tiled=True)
    sent, kept = partial(mine ^ 3, mine ^ 2, resident=True)
    far = added(kept, exchange(sent, 1))
    far_got = exchange(far, 2)
    sent, kept = partial(mine ^ 1, mine, after=far)
    near = kept.astype(F32) + exchange(sent, 1).astype(F32)
    return (near + far_got.astype(F32)).astype(BF16)


def solution(mesh):
    return jax.shard_map(
        on_device,
        mesh=mesh,
        in_specs=(
            P(("parts", "seq"), "head"),
            P(("parts", "seq"), "head"),
            P(("parts", "seq"), "head"),
            P(("parts", "seq"), "head"),
            P("head", ("parts", "seq")),
            P("head", ("parts", "seq")),
            P(None, None, "head"),
            P(),
            P("head", None),
            P("parts"),
        ),
        out_specs=P(("parts", "seq", "head"), None),
        check_vma=False,
    )
```

```python
import functools

import jax
import jax.numpy as jnp
import numpy as np
from jax import lax
from jax.experimental import pallas as pl
from jax.experimental.pallas import tpu as pltpu
from jax.sharding import PartitionSpec as P

CHUNK = 128
RIM = 16
GROUP = 8
SUBS = 2
F32 = jnp.float32
BF16 = jnp.bfloat16
NN = (((1,), (0,)), ((), ()))
NT = (((1,), (1,)), ((), ()))


def mm(left, right, dims=NN):
    return lax.dot_general(left, right, dims, preferred_element_type=F32)


def exact(left, right, dims=NN):
    return lax.dot_general(
        left, right, dims, precision=lax.Precision.HIGHEST, preferred_element_type=F32
    )


def sigmoid(x):
    return 0.5 + 0.5 * jnp.tanh(0.5 * x)


def conv_silu(raw, rim, taps):
    rows, n = raw.shape[0], rim.shape[0]
    padded = jnp.concatenate([rim, raw], axis=0)
    before = pltpu.roll(padded, 1, 0)
    old = pltpu.roll(taps[1:2] * padded + taps[0:1] * before, 2, 0)
    total = (taps[3:4] * padded + taps[2:3] * before + old)[n:]
    return total * sigmoid(total)


def unit(x, scale):
    return (x * (lax.rsqrt(jnp.sum(x * x, axis=-1, keepdims=True) + 1e-06) * scale)).astype(BF16)


def placed(*arrays):
    return [pltpu.with_memory_space_constraint(x, pltpu.HBM) for x in arrays]


def positions(c):
    return (
        lax.broadcasted_iota(jnp.int32, (c, c), 0),
        lax.broadcasted_iota(jnp.int32, (c, c), 1),
    )


def channels(rim_ref, ref, prev_ref, taps_ref, which, sl, first):
    raw = ref[:, sl].astype(F32)
    rim = jnp.where(first, rim_ref[which, :, sl].astype(F32), prev_ref[:, sl].astype(F32))
    return conv_silu(raw, rim[-8:], taps_ref[which, :, sl])


def summary_kernel(
    rim_ref, k_ref, v_ref, kp_ref, vp_ref, dec_ref, wr_ref, taps_ref, mask_ref,
    keys_ref, fresh_ref, start_ref, summary_ref, state_ref,
):
    step = pl.program_id(0)
    c = CHUNK
    subs = k_ref.shape[0] // c
    heads = dec_ref.shape[0]
    width = k_ref.shape[1] // heads

    @pl.when(step == 0)
    def _():
        rows = lax.broadcasted_iota(jnp.int32, (width, 2 * width), 0)
        cols = lax.broadcasted_iota(jnp.int32, (width, 2 * width), 1)
        eye = jnp.where(rows == cols, 1.0, 0.0).astype(F32)
        for h in range(heads):
            state_ref[h] = eye

    ri, ci = positions(c)
    tril = jnp.where(ci <= ri, 1.0, 0.0).astype(F32)
    eye = jnp.where(ci == ri, 1.0, 0.0).astype(F32)
    first = step == 0
    dec = [dec_ref[:, s * c : (s + 1) * c] for s in range(subs)]
    wr = [wr_ref[:, s * c : (s + 1) * c] for s in range(subs)]
    cum_row = [exact(x, tril, NT) for x in dec]
    cum_col = [exact(tril, x, NT) for x in dec]
    wr_col = [exact(eye, x, NT) for x in wr]
    last = [x[:, c - 1 : c] for x in cum_row]
    log_col = [cum_col[s] + jnp.log(wr_col[s]) for s in range(subs)]
    drop_col = [-wr_col[s] * jnp.exp(cum_col[s]) for s in range(subs)]
    kout_row = [jnp.exp(last[s] - cum_row[s]) for s in range(subs)]
    last_decay = [jnp.exp(x) for x in last]

    units = [(s, h) for s in range(subs) for h in range(heads)]
    n = range(len(units))

    def lanes(h):
        return slice(h * width, (h + 1) * width)

    def row(x, i):
        s, h = units[i]
        return x[s][h : h + 1, :]

    def col(x, i):
        s, h = units[i]
        return x[s][:, h : h + 1]

    def split(x):
        return {(s, h): x[h][s * c : (s + 1) * c] for s, h in units}

    k_all = [unit(channels(rim_ref, k_ref, kp_ref, taps_ref, 1, lanes(h), first), 1.0) for h in range(heads)]
    for h in range(heads):
        keys_ref[:, lanes(h)] = k_all[h]
    k = [k_all[h][s * c : (s + 1) * c] for s, h in units]
    gram = [mm(x, x, NT) for x in k]
    low = []
    for i in n:
        decay = jnp.exp(col(log_col, i) - row(cum_row, i))
        low.append(jnp.where(ci < ri, gram[i] * decay, 0.0).astype(BF16))
    inv = [eye.astype(BF16) - x * mask_ref[0] for x in low]
    level = 1
    while (1 << level) < c:
        mask = mask_ref[level]
        inner = [mm(low[i] * mask, inv[i]).astype(BF16) for i in n]
        inv = [inv[i] - mm(inv[i], inner[i]).astype(BF16) for i in n]
        level += 1
    v_all = [channels(rim_ref, v_ref, vp_ref, taps_ref, 2, lanes(h), first).astype(BF16) for h in range(heads)]
    v = [v_all[h][s * c : (s + 1) * c] for s, h in units]
    kf = [x.astype(F32) for x in k]
    sides = [
        jnp.concatenate(
            [
                (kf[i] * col(drop_col, i)).astype(BF16),
                (v[i].astype(F32) * col(wr_col, i)).astype(BF16),
            ],
            axis=1,
        )
        for i in n
    ]
    mixed = [mm(inv[i], sides[i]) for i in n]
    k_out = [(kf[i].T * row(kout_row, i)).astype(BF16) for i in n]
    for s in range(subs):
        at = s * heads
        start = [state_ref[h].astype(BF16) for h in range(heads)]
        for h in range(heads):
            start_ref[s, h] = start[h]
        read = [mm(mixed[at + h][:, :width].astype(BF16), start[h]) for h in range(heads)]
        fresh = [
            jnp.concatenate(
                [read[h][:, :width], mixed[at + h][:, width:] + read[h][:, width:]], axis=1
            ).astype(BF16)
            for h in range(heads)
        ]
        for h in range(heads):
            fresh_ref[s * c : (s + 1) * c, 2 * h * width : 2 * (h + 1) * width] = fresh[h]
        both = [mm(k_out[at + h], fresh[h]) for h in range(heads)]
        for h in range(heads):
            state_ref[h] = last_decay[s][h : h + 1, :] * state_ref[h] + both[h]

    @pl.when(step == pl.num_programs(0) - 1)
    def _():
        summary_ref[...] = state_ref[...].astype(BF16)


def local_kernel(
    begin, rim_ref, q_ref, qp_ref, keys_ref, fresh_ref, start_ref, dec_ref, taps_ref, *rest
):
    local_ref, qeff_ref = rest[-2:]
    step = pl.program_id(0) + begin
    c = q_ref.shape[0]
    heads = dec_ref.shape[0]
    width = q_ref.shape[1] // heads
    ri, ci = positions(c)
    tril = jnp.where(ci <= ri, 1.0, 0.0).astype(F32)
    dec = dec_ref[...]
    cum_row = exact(dec, tril, NT)
    cum_col = exact(tril, dec, NT)
    gamma_col = jnp.exp(cum_col)
    first = step == 0
    for g in range(0, heads, GROUP):
        hs = range(g, g + GROUP)
        sls = [slice(h * width, (h + 1) * width) for h in hs]
        n = range(GROUP)
        q = [unit(channels(rim_ref, q_ref, qp_ref, taps_ref, 0, sl, first), width ** -0.5) for sl in sls]
        gram = [mm(q[i], keys_ref[:, sls[i]], NT) for i in n]
        for i in n:
            h = hs[i]
            gap = cum_col[:, h : h + 1] - cum_row[h : h + 1, :]
            scores = jnp.where(ci <= ri, gram[i] * jnp.exp(gap), 0.0).astype(BF16)
            q_in = (q[i].astype(F32) * gamma_col[:, h : h + 1]).astype(BF16)
            out = mm(
                jnp.concatenate([q_in, scores], axis=1),
                jnp.concatenate(
                    [start_ref[0, h], fresh_ref[:, 2 * h * width : 2 * (h + 1) * width]], axis=0
                ),
            )
            qeff_ref[:, sls[i]] = out[:, :width].astype(BF16)
            local_ref[:, sls[i]] = out[:, width:].astype(BF16)


def level_masks(c):
    r = np.arange(c)
    differ = r[:, None] ^ r[None, :]
    lower = r[:, None] > r[None, :]
    levels = []
    size = 1
    while size < c:
        levels.append(lower & (differ >= size) & (differ < 2 * size))
        size *= 2
    return jnp.asarray(np.stack(levels), BF16)


def front(rim, query_raw, key_raw, value_raw, log_decay, write_strength, conv_weight):
    rows, channel_count = query_raw.shape
    heads = log_decay.shape[0]
    width = channel_count // heads
    c = CHUNK
    steps = rows // c
    per = c // RIM
    masks = level_masks(c)
    block = pl.BlockSpec((c, channel_count), lambda i: (i, 0))
    wide = pl.BlockSpec((c, 2 * channel_count), lambda i: (i, 0))
    prev = pl.BlockSpec((RIM, channel_count), lambda i: (jnp.maximum(i * per - 1, 0), 0))
    gates = pl.BlockSpec((heads, c), lambda i: (0, i))
    rims = pl.BlockSpec((3, RIM, channel_count), lambda i: (0, 0, 0))
    taps = pl.BlockSpec((3, 4, channel_count), lambda i: (0, 0, 0))
    starts = pl.BlockSpec((1, heads, width, 2 * width), lambda i: (i, 0, 0, 0))
    params = pltpu.CompilerParams(vmem_limit_bytes=48 << 20)
    subs = SUBS if steps % SUBS == 0 else 1
    big = pl.BlockSpec((subs * c, channel_count), lambda i: (i, 0))
    keys, fresh, start, summary = pl.pallas_call(
        summary_kernel,
        grid=(steps // subs,),
        in_specs=[
            rims, big, big,
            pl.BlockSpec((RIM, channel_count), lambda i: (jnp.maximum(i * per * subs - 1, 0), 0)),
            pl.BlockSpec((RIM, channel_count), lambda i: (jnp.maximum(i * per * subs - 1, 0), 0)),
            pl.BlockSpec((heads, subs * c), lambda i: (0, i)),
            pl.BlockSpec((heads, subs * c), lambda i: (0, i)), taps,
            pl.BlockSpec(masks.shape, lambda i: (0, 0, 0)),
        ],
        out_specs=[
            big,
            pl.BlockSpec((subs * c, 2 * channel_count), lambda i: (i, 0)),
            pl.BlockSpec((subs, heads, width, 2 * width), lambda i: (i, 0, 0, 0)),
            pl.BlockSpec((heads, width, 2 * width), lambda i: (0, 0, 0)),
        ],
        out_shape=[
            pltpu.HBM((rows, channel_count), BF16),
            pltpu.HBM((rows, 2 * channel_count), BF16),
            pltpu.HBM((steps, heads, width, 2 * width), BF16),
            jax.ShapeDtypeStruct((heads, width, 2 * width), BF16),
        ],
        scratch_shapes=[pltpu.VMEM((heads, width, 2 * width), F32)],
        compiler_params=params,
        name="summary",
    )(rim, *placed(key_raw, value_raw, key_raw, value_raw, log_decay, write_strength, conv_weight, masks))
    first = steps // 3

    def local_part(begin, count, done, rim, keys, fresh, start):
        def at(spec):
            return pl.BlockSpec(spec.block_shape, lambda i: spec.index_map(i + begin))

        return pl.pallas_call(
            functools.partial(local_kernel, begin),
            grid=(count,),
            in_specs=[rims, *map(at, (block, prev, block, wide, starts, gates)), taps]
            + [pl.BlockSpec(memory_space=pl.ANY)] * len(done),
            out_specs=[at(block), at(block)],
            out_shape=[
                pltpu.HBM((rows, channel_count), BF16),
                pltpu.HBM((rows, channel_count), BF16),
            ],
            input_output_aliases={8 + i: i for i in range(len(done))},
            compiler_params=params,
            name="local",
        )(rim, *placed(query_raw, query_raw, keys, fresh, start, log_decay, conv_weight, *done))

    def early():
        return local_part(0, first, (), rim, keys, fresh, start)

    def late(done):
        return local_part(first, steps - first, done, rim, keys, fresh, start)

    return early, late, summary


def out_kernel(
    info_ref, state_ref, local_ref, qeff_ref, gate_ref, gain_ref, weight_ref, *out_refs
):
    step = pl.program_id(0)
    heads, width = state_ref.shape[0], state_ref.shape[1]
    rows = local_ref.shape[0]
    base = info_ref[0] + info_ref[2 + step] * rows
    valid = base + lax.broadcasted_iota(jnp.int32, (rows, width), 0) < info_ref[1]
    gated = []
    for h in range(heads):
        sl = slice(h * width, (h + 1) * width)
        o = local_ref[:, sl].astype(F32) + mm(qeff_ref[:, sl], state_ref[h])
        norm = lax.rsqrt(jnp.mean(o * o, axis=-1, keepdims=True) + 1e-06)
        g = gate_ref[:, sl].astype(F32)
        o = o * norm * gain_ref[...] * (g * sigmoid(g))
        gated.append(jnp.where(valid, o, 0.0).astype(BF16))
    result = mm(jnp.concatenate(gated, axis=1), weight_ref[...]).astype(BF16)
    for i, out_ref in enumerate(out_refs):

        @pl.when(step == i)
        def _(out_ref=out_ref):
            out_ref[...] = result


def passed_along(block, axis, distance):
    devices = range(lax.axis_size(axis))
    route = [(i - distance, i) for i in devices if i - distance in devices]
    return lax.ppermute(block, axis, route)


def ends_kernel(q_ref, k_ref, v_ref, out_ref):
    out_ref[0] = q_ref[...]
    out_ref[1] = k_ref[...]
    out_ref[2] = v_ref[...]


def ends(*arrays):
    rows, channel_count = arrays[0].shape
    last = rows // RIM - 1
    return pl.pallas_call(
        ends_kernel,
        grid=(1,),
        in_specs=[pl.BlockSpec((RIM, channel_count), lambda i: (last, 0))] * 3,
        out_specs=pl.BlockSpec((3, RIM, channel_count), lambda i: (0, 0, 0)),
        out_shape=jax.ShapeDtypeStruct((3, RIM, channel_count), BF16),
        name="ends",
    )(*placed(*arrays))


def carried_in(summary, axis, early, late):
    width = summary.shape[1]
    count = lax.axis_size(axis)
    move, own = summary[:, :, :width], summary[:, :, width:]

    def apply(a, b, s):
        return jnp.einsum("hij,hjk->hik", a, s, preferred_element_type=F32) + b.astype(F32)

    if count == 4:
        first = lax.ppermute(own, axis, [(0, 1)])
        third = lax.ppermute(summary, axis, [(2, 3)])
        done = early()
        first, done = lax.optimization_barrier((first, done))
        pair = apply(move, own, first).astype(BF16)
        far = lax.ppermute(pair, axis, [(1, 3)])
        near = lax.ppermute(pair, axis, [(1, 2)])
        done, pair = lax.optimization_barrier((done, pair))
        done = late(done)
        state = apply(third[:, :, :width], third[:, :, width:], far)
        return (state + near.astype(F32) + first.astype(F32)).astype(BF16), *done
    state = passed_along(own, axis, 1)
    for _ in range(count - 2):
        state = passed_along(apply(move, own, state).astype(BF16), axis, 1)
    return state, *late(early())


def on_device(
    query_raw, key_raw, value_raw, out_gate, log_decay, write_strength,
    conv_weight, norm_gain, out_weight, history_end,
):
    rows, channel_count = query_raw.shape
    heads = log_decay.shape[0]
    width = channel_count // heads
    rim = passed_along(ends(query_raw, key_raw, value_raw), "seq", 1)
    early, late, summary = front(
        rim, query_raw, key_raw, value_raw, log_decay, write_strength, conv_weight
    )
    state, local, qeff = carried_in(summary, "seq", early, late)
    owners = lax.axis_size("head")
    mine = lax.axis_index("head")
    dim = out_weight.shape[1]
    start = lax.axis_index("seq") * rows
    gain = norm_gain.reshape(1, width)

    def partial(*blocks, after=None, resident=False):
        tile = rows // owners
        info = jnp.stack([start, history_end[0], *blocks]).astype(jnp.int32)
        if after is not None:
            info, after = lax.optimization_barrier((info, after))
        tiles = pl.BlockSpec((tile, channel_count), lambda i, s: (s[2 + i], 0))
        weight = out_weight if resident else placed(out_weight)[0]
        return pl.pallas_call(
            out_kernel,
            grid_spec=pltpu.PrefetchScalarGridSpec(
                num_scalar_prefetch=1,
                grid=(len(blocks),),
                in_specs=[
                    pl.BlockSpec((heads, width, width), lambda i, s: (0, 0, 0)),
                    tiles, tiles, tiles,
                    pl.BlockSpec((1, width), lambda i, s: (0, 0)),
                    pl.BlockSpec(memory_space=pltpu.VMEM)
                    if resident
                    else pl.BlockSpec((channel_count, dim), lambda i, s: (0, 0)),
                ],
                out_specs=[pl.BlockSpec((tile, dim), lambda i, s: (0, 0))] * len(blocks),
            ),
            out_shape=[jax.ShapeDtypeStruct((tile, dim), BF16)] * len(blocks),
            compiler_params=pltpu.CompilerParams(vmem_limit_bytes=24 << 20),
            name="outputs",
        )(info, state, *placed(local, qeff, out_gate, gain), weight)

    def exchange(block, bit):
        return lax.ppermute(block, "head", [(i, i ^ bit) for i in range(owners)])

    def added(a, b):
        return (a.astype(F32) + b.astype(F32)).astype(BF16)

    if owners != 4:
        blocks = jnp.concatenate(partial(*range(owners)), axis=0)
        return lax.psum_scatter(blocks, "head", scatter_dimension=0, tiled=True)
    sent, kept = partial(mine ^ 3, mine ^ 2, resident=True)
    far = added(kept, exchange(sent, 1))
    far_got = exchange(far, 2)
    sent, kept = partial(mine ^ 1, mine, after=far)
    near = kept.astype(F32) + exchange(sent, 1).astype(F32)
    return (near + far_got.astype(F32)).astype(BF16)


def solution(mesh):
    return jax.shard_map(
        on_device,
        mesh=mesh,
        in_specs=(
            P(("parts", "seq"), "head"),
            P(("parts", "seq"), "head"),
            P(("parts", "seq"), "head"),
            P(("parts", "seq"), "head"),
            P("head", ("parts", "seq")),
            P("head", ("parts", "seq")),
            P(None, None, "head"),
            P(),
            P("head", None),
            P("parts"),
        ),
        out_specs=P(("parts", "seq", "head"), None),
        check_vma=False,
    )
```

```python
import functools

import jax
import jax.numpy as jnp
import numpy as np
from jax import lax
from jax.experimental import pallas as pl
from jax.experimental.pallas import tpu as pltpu
from jax.sharding import PartitionSpec as P

CHUNK = 128
RIM = 16
GROUP = 8
SUBS = 2
F32 = jnp.float32
BF16 = jnp.bfloat16
NN = (((1,), (0,)), ((), ()))
NT = (((1,), (1,)), ((), ()))


def mm(left, right, dims=NN):
    return lax.dot_general(left, right, dims, preferred_element_type=F32)


def exact(left, right, dims=NN):
    return lax.dot_general(
        left, right, dims, precision=lax.Precision.HIGHEST, preferred_element_type=F32
    )


def sigmoid(x):
    return 0.5 + 0.5 * jnp.tanh(0.5 * x)


def conv_silu(raw, rim, taps):
    rows, n = raw.shape[0], rim.shape[0]
    padded = jnp.concatenate([rim, raw], axis=0)
    before = pltpu.roll(padded, 1, 0)
    old = pltpu.roll(taps[1:2] * padded + taps[0:1] * before, 2, 0)
    total = (taps[3:4] * padded + taps[2:3] * before + old)[n:]
    return total * sigmoid(total)


def unit(x, scale):
    return (x * (lax.rsqrt(jnp.sum(x * x, axis=-1, keepdims=True) + 1e-06) * scale)).astype(BF16)


def placed(*arrays):
    return [pltpu.with_memory_space_constraint(x, pltpu.HBM) for x in arrays]


def positions(c):
    return (
        lax.broadcasted_iota(jnp.int32, (c, c), 0),
        lax.broadcasted_iota(jnp.int32, (c, c), 1),
    )


def channels(rim_ref, ref, prev_ref, taps_ref, which, sl, first):
    raw = ref[:, sl].astype(F32)
    rim = jnp.where(first, rim_ref[which, :, sl].astype(F32), prev_ref[:, sl].astype(F32))
    return conv_silu(raw, rim[-8:], taps_ref[which, :, sl])


def summary_kernel(
    rim_ref, k_ref, v_ref, kp_ref, vp_ref, dec_ref, wr_ref, taps_ref, mask_ref,
    keys_ref, fresh_ref, start_ref, summary_ref, state_ref,
):
    step = pl.program_id(0)
    c = CHUNK
    subs = k_ref.shape[0] // c
    heads = dec_ref.shape[0]
    width = k_ref.shape[1] // heads

    @pl.when(step == 0)
    def _():
        rows = lax.broadcasted_iota(jnp.int32, (width, 2 * width), 0)
        cols = lax.broadcasted_iota(jnp.int32, (width, 2 * width), 1)
        eye = jnp.where(rows == cols, 1.0, 0.0).astype(F32)
        for h in range(heads):
            state_ref[h] = eye

    ri, ci = positions(c)
    tril = jnp.where(ci <= ri, 1.0, 0.0).astype(F32)
    eye = jnp.where(ci == ri, 1.0, 0.0).astype(F32)
    first = step == 0
    dec = [dec_ref[:, s * c : (s + 1) * c] for s in range(subs)]
    wr = [wr_ref[:, s * c : (s + 1) * c] for s in range(subs)]
    cum_row = [exact(x, tril, NT) for x in dec]
    cum_col = [exact(tril, x, NT) for x in dec]
    wr_col = [exact(eye, x, NT) for x in wr]
    last = [x[:, c - 1 : c] for x in cum_row]
    log_col = [cum_col[s] + jnp.log(wr_col[s]) for s in range(subs)]
    drop_col = [-wr_col[s] * jnp.exp(cum_col[s]) for s in range(subs)]
    kout_row = [jnp.exp(last[s] - cum_row[s]) for s in range(subs)]
    last_decay = [jnp.exp(x) for x in last]

    units = [(s, h) for s in range(subs) for h in range(heads)]
    n = range(len(units))

    def lanes(h):
        return slice(h * width, (h + 1) * width)

    def row(x, i):
        s, h = units[i]
        return x[s][h : h + 1, :]

    def col(x, i):
        s, h = units[i]
        return x[s][:, h : h + 1]

    def split(x):
        return {(s, h): x[h][s * c : (s + 1) * c] for s, h in units}

    k_all = [unit(channels(rim_ref, k_ref, kp_ref, taps_ref, 1, lanes(h), first), 1.0) for h in range(heads)]
    for h in range(heads):
        keys_ref[:, lanes(h)] = k_all[h]
    k = [k_all[h][s * c : (s + 1) * c] for s, h in units]
    gram = [mm(x, x, NT) for x in k]
    low = []
    for i in n:
        decay = jnp.exp(col(log_col, i) - row(cum_row, i))
        low.append(jnp.where(ci < ri, gram[i] * decay, 0.0).astype(BF16))
    inv = [eye.astype(BF16) - x * mask_ref[0] for x in low]
    level = 1
    while (1 << level) < c:
        mask = mask_ref[level]
        inner = [mm(low[i] * mask, inv[i]).astype(BF16) for i in n]
        inv = [inv[i] - mm(inv[i], inner[i]).astype(BF16) for i in n]
        level += 1
    v_all = [channels(rim_ref, v_ref, vp_ref, taps_ref, 2, lanes(h), first).astype(BF16) for h in range(heads)]
    v = [v_all[h][s * c : (s + 1) * c] for s, h in units]
    kf = [x.astype(F32) for x in k]
    sides = [
        jnp.concatenate(
            [
                (kf[i] * col(drop_col, i)).astype(BF16),
                (v[i].astype(F32) * col(wr_col, i)).astype(BF16),
            ],
            axis=1,
        )
        for i in n
    ]
    mixed = [mm(inv[i], sides[i]) for i in n]
    k_out = [(kf[i].T * row(kout_row, i)).astype(BF16) for i in n]
    for s in range(subs):
        at = s * heads
        start = [state_ref[h].astype(BF16) for h in range(heads)]
        for h in range(heads):
            start_ref[s, h] = start[h]
        read = [mm(mixed[at + h][:, :width].astype(BF16), start[h]) for h in range(heads)]
        fresh = [
            jnp.concatenate(
                [read[h][:, :width], mixed[at + h][:, width:] + read[h][:, width:]], axis=1
            ).astype(BF16)
            for h in range(heads)
        ]
        for h in range(heads):
            fresh_ref[s * c : (s + 1) * c, 2 * h * width : 2 * (h + 1) * width] = fresh[h]
        both = [mm(k_out[at + h], fresh[h]) for h in range(heads)]
        for h in range(heads):
            state_ref[h] = last_decay[s][h : h + 1, :] * state_ref[h] + both[h]

    @pl.when(step == pl.num_programs(0) - 1)
    def _():
        summary_ref[...] = state_ref[...].astype(BF16)


def local_kernel(
    begin, rim_ref, q_ref, qp_ref, keys_ref, fresh_ref, start_ref, dec_ref, taps_ref, *rest
):
    local_ref, qeff_ref = rest[-2:]
    step = pl.program_id(0) + begin
    c = q_ref.shape[0]
    heads = dec_ref.shape[0]
    width = q_ref.shape[1] // heads
    ri, ci = positions(c)
    tril = jnp.where(ci <= ri, 1.0, 0.0).astype(F32)
    dec = dec_ref[...]
    cum_row = exact(dec, tril, NT)
    cum_col = exact(tril, dec, NT)
    gamma_col = jnp.exp(cum_col)
    first = step == 0
    for g in range(0, heads, GROUP):
        hs = range(g, g + GROUP)
        sls = [slice(h * width, (h + 1) * width) for h in hs]
        n = range(GROUP)
        q = [unit(channels(rim_ref, q_ref, qp_ref, taps_ref, 0, sl, first), width ** -0.5) for sl in sls]
        gram = [mm(q[i], keys_ref[:, sls[i]], NT) for i in n]
        for i in n:
            h = hs[i]
            gap = cum_col[:, h : h + 1] - cum_row[h : h + 1, :]
            scores = jnp.where(ci <= ri, gram[i] * jnp.exp(gap), 0.0).astype(BF16)
            q_in = (q[i].astype(F32) * gamma_col[:, h : h + 1]).astype(BF16)
            out = mm(
                jnp.concatenate([q_in, scores], axis=1),
                jnp.concatenate(
                    [start_ref[0, h], fresh_ref[:, 2 * h * width : 2 * (h + 1) * width]], axis=0
                ),
            )
            qeff_ref[:, sls[i]] = out[:, :width].astype(BF16)
            local_ref[:, sls[i]] = out[:, width:].astype(BF16)


def level_masks(c):
    r = np.arange(c)
    differ = r[:, None] ^ r[None, :]
    lower = r[:, None] > r[None, :]
    levels = []
    size = 1
    while size < c:
        levels.append(lower & (differ >= size) & (differ < 2 * size))
        size *= 2
    return jnp.asarray(np.stack(levels), BF16)


def front(rim, query_raw, key_raw, value_raw, log_decay, write_strength, conv_weight):
    rows, channel_count = query_raw.shape
    heads = log_decay.shape[0]
    width = channel_count // heads
    c = CHUNK
    steps = rows // c
    per = c // RIM
    masks = level_masks(c)
    block = pl.BlockSpec((c, channel_count), lambda i: (i, 0))
    wide = pl.BlockSpec((c, 2 * channel_count), lambda i: (i, 0))
    prev = pl.BlockSpec((RIM, channel_count), lambda i: (jnp.maximum(i * per - 1, 0), 0))
    gates = pl.BlockSpec((heads, c), lambda i: (0, i))
    rims = pl.BlockSpec((3, RIM, channel_count), lambda i: (0, 0, 0))
    taps = pl.BlockSpec((3, 4, channel_count), lambda i: (0, 0, 0))
    starts = pl.BlockSpec((1, heads, width, 2 * width), lambda i: (i, 0, 0, 0))
    params = pltpu.CompilerParams(vmem_limit_bytes=48 << 20)
    subs = SUBS if steps % SUBS == 0 else 1
    big = pl.BlockSpec((subs * c, channel_count), lambda i: (i, 0))
    keys, fresh, start, summary = pl.pallas_call(
        summary_kernel,
        grid=(steps // subs,),
        in_specs=[
            rims, big, big,
            pl.BlockSpec((RIM, channel_count), lambda i: (jnp.maximum(i * per * subs - 1, 0), 0)),
            pl.BlockSpec((RIM, channel_count), lambda i: (jnp.maximum(i * per * subs - 1, 0), 0)),
            pl.BlockSpec((heads, subs * c), lambda i: (0, i)),
            pl.BlockSpec((heads, subs * c), lambda i: (0, i)), taps,
            pl.BlockSpec(masks.shape, lambda i: (0, 0, 0)),
        ],
        out_specs=[
            big,
            pl.BlockSpec((subs * c, 2 * channel_count), lambda i: (i, 0)),
            pl.BlockSpec((subs, heads, width, 2 * width), lambda i: (i, 0, 0, 0)),
            pl.BlockSpec((heads, width, 2 * width), lambda i: (0, 0, 0)),
        ],
        out_shape=[
            pltpu.HBM((rows, channel_count), BF16),
            pltpu.HBM((rows, 2 * channel_count), BF16),
            pltpu.HBM((steps, heads, width, 2 * width), BF16),
            jax.ShapeDtypeStruct((heads, width, 2 * width), BF16),
        ],
        scratch_shapes=[pltpu.VMEM((heads, width, 2 * width), F32)],
        compiler_params=params,
        name="summary",
    )(rim, *placed(key_raw, value_raw, key_raw, value_raw, log_decay, write_strength, conv_weight, masks))
    first = steps // 3

    def local_part(begin, count, done, rim, keys, fresh, start):
        def at(spec):
            return pl.BlockSpec(spec.block_shape, lambda i: spec.index_map(i + begin))

        return pl.pallas_call(
            functools.partial(local_kernel, begin),
            grid=(count,),
            in_specs=[rims, *map(at, (block, prev, block, wide, starts, gates)), taps]
            + [pl.BlockSpec(memory_space=pl.ANY)] * len(done),
            out_specs=[at(block), at(block)],
            out_shape=[
                pltpu.HBM((rows, channel_count), BF16),
                pltpu.HBM((rows, channel_count), BF16),
            ],
            input_output_aliases={8 + i: i for i in range(len(done))},
            compiler_params=params,
            name="local",
        )(rim, *placed(query_raw, query_raw, keys, fresh, start, log_decay, conv_weight, *done))

    def early():
        return local_part(0, first, (), rim, keys, fresh, start)

    def late(done):
        return local_part(first, steps - first, done, rim, keys, fresh, start)

    return early, late, summary


def out_kernel(
    info_ref, state_ref, local_ref, qeff_ref, gate_ref, gain_ref, weight_ref, *out_refs
):
    step = pl.program_id(0)
    heads, width = state_ref.shape[0], state_ref.shape[1]
    rows = local_ref.shape[0]
    base = info_ref[0] + info_ref[2 + step] * rows
    valid = base + lax.broadcasted_iota(jnp.int32, (rows, width), 0) < info_ref[1]
    gated = []
    for h in range(heads):
        sl = slice(h * width, (h + 1) * width)
        o = local_ref[:, sl].astype(F32) + mm(qeff_ref[:, sl], state_ref[h])
        norm = lax.rsqrt(jnp.mean(o * o, axis=-1, keepdims=True) + 1e-06)
        g = gate_ref[:, sl].astype(F32)
        o = o * norm * gain_ref[...] * (g * sigmoid(g))
        gated.append(jnp.where(valid, o, 0.0).astype(BF16))
    result = mm(jnp.concatenate(gated, axis=1), weight_ref[...]).astype(BF16)
    for i, out_ref in enumerate(out_refs):

        @pl.when(step == i)
        def _(out_ref=out_ref):
            out_ref[...] = result


def passed_along(block, axis, distance):
    devices = range(lax.axis_size(axis))
    route = [(i - distance, i) for i in devices if i - distance in devices]
    return lax.ppermute(block, axis, route)


def ends_kernel(q_ref, k_ref, v_ref, out_ref):
    out_ref[0] = q_ref[...]
    out_ref[1] = k_ref[...]
    out_ref[2] = v_ref[...]


def ends(*arrays):
    rows, channel_count = arrays[0].shape
    last = rows // RIM - 1
    return pl.pallas_call(
        ends_kernel,
        grid=(1,),
        in_specs=[pl.BlockSpec((RIM, channel_count), lambda i: (last, 0))] * 3,
        out_specs=pl.BlockSpec((3, RIM, channel_count), lambda i: (0, 0, 0)),
        out_shape=jax.ShapeDtypeStruct((3, RIM, channel_count), BF16),
        name="ends",
    )(*placed(*arrays))


def carried_in(summary, axis, early, late):
    width = summary.shape[1]
    count = lax.axis_size(axis)
    move, own = summary[:, :, :width], summary[:, :, width:]

    def apply(a, b, s):
        return jnp.einsum("hij,hjk->hik", a, s, preferred_element_type=F32) + b.astype(F32)

    if count == 4:
        first = lax.ppermute(own, axis, [(0, 1)])
        third = lax.ppermute(summary, axis, [(2, 3)])
        done = early()
        first, done = lax.optimization_barrier((first, done))
        pair = apply(move, own, first).astype(BF16)
        near = lax.ppermute(pair, axis, [(1, 2)])
        far = lax.ppermute(pair, axis, [(1, 3)])
        done, pair = lax.optimization_barrier((done, pair))
        done = late(done)
        state = apply(third[:, :, :width], third[:, :, width:], far)
        return (state + near.astype(F32) + first.astype(F32)).astype(BF16), *done
    state = passed_along(own, axis, 1)
    for _ in range(count - 2):
        state = passed_along(apply(move, own, state).astype(BF16), axis, 1)
    return state, *late(early())


def on_device(
    query_raw, key_raw, value_raw, out_gate, log_decay, write_strength,
    conv_weight, norm_gain, out_weight, history_end,
):
    rows, channel_count = query_raw.shape
    heads = log_decay.shape[0]
    width = channel_count // heads
    rim = passed_along(ends(query_raw, key_raw, value_raw), "seq", 1)
    early, late, summary = front(
        rim, query_raw, key_raw, value_raw, log_decay, write_strength, conv_weight
    )
    state, local, qeff = carried_in(summary, "seq", early, late)
    owners = lax.axis_size("head")
    mine = lax.axis_index("head")
    dim = out_weight.shape[1]
    start = lax.axis_index("seq") * rows
    gain = norm_gain.reshape(1, width)

    def partial(*blocks, after=None, resident=False):
        tile = rows // owners
        info = jnp.stack([start, history_end[0], *blocks]).astype(jnp.int32)
        if after is not None:
            info, after = lax.optimization_barrier((info, after))
        tiles = pl.BlockSpec((tile, channel_count), lambda i, s: (s[2 + i], 0))
        weight = out_weight if resident else placed(out_weight)[0]
        return pl.pallas_call(
            out_kernel,
            grid_spec=pltpu.PrefetchScalarGridSpec(
                num_scalar_prefetch=1,
                grid=(len(blocks),),
                in_specs=[
                    pl.BlockSpec((heads, width, width), lambda i, s: (0, 0, 0)),
                    tiles, tiles, tiles,
                    pl.BlockSpec((1, width), lambda i, s: (0, 0)),
                    pl.BlockSpec(memory_space=pltpu.VMEM)
                    if resident
                    else pl.BlockSpec((channel_count, dim), lambda i, s: (0, 0)),
                ],
                out_specs=[pl.BlockSpec((tile, dim), lambda i, s: (0, 0))] * len(blocks),
            ),
            out_shape=[jax.ShapeDtypeStruct((tile, dim), BF16)] * len(blocks),
            compiler_params=pltpu.CompilerParams(vmem_limit_bytes=24 << 20),
            name="outputs",
        )(info, state, *placed(local, qeff, out_gate, gain), weight)

    def exchange(block, bit):
        return lax.ppermute(block, "head", [(i, i ^ bit) for i in range(owners)])

    def added(a, b):
        return (a.astype(F32) + b.astype(F32)).astype(BF16)

    if owners != 4:
        blocks = jnp.concatenate(partial(*range(owners)), axis=0)
        return lax.psum_scatter(blocks, "head", scatter_dimension=0, tiled=True)
    sent, kept = partial(mine ^ 3, mine ^ 2, resident=True)
    far = added(kept, exchange(sent, 1))
    far_got = exchange(far, 2)
    sent, kept = partial(mine ^ 1, mine, after=far)
    near = kept.astype(F32) + exchange(sent, 1).astype(F32)
    return (near + far_got.astype(F32)).astype(BF16)


def solution(mesh):
    return jax.shard_map(
        on_device,
        mesh=mesh,
        in_specs=(
            P(("parts", "seq"), "head"),
            P(("parts", "seq"), "head"),
            P(("parts", "seq"), "head"),
            P(("parts", "seq"), "head"),
            P("head", ("parts", "seq")),
            P("head", ("parts", "seq")),
            P(None, None, "head"),
            P(),
            P("head", None),
            P("parts"),
        ),
        out_specs=P(("parts", "seq", "head"), None),
        check_vma=False,
    )
```

```python
import functools

import jax
import jax.numpy as jnp
import numpy as np
from jax import lax
from jax.experimental import pallas as pl
from jax.experimental.pallas import tpu as pltpu
from jax.sharding import PartitionSpec as P

CHUNK = 128
RIM = 16
GROUP = 8
SUBS = 2
F32 = jnp.float32
BF16 = jnp.bfloat16
NN = (((1,), (0,)), ((), ()))
NT = (((1,), (1,)), ((), ()))


def mm(left, right, dims=NN):
    return lax.dot_general(left, right, dims, preferred_element_type=F32)


def exact(left, right, dims=NN):
    return lax.dot_general(
        left, right, dims, precision=lax.Precision.HIGHEST, preferred_element_type=F32
    )


def sigmoid(x):
    return 0.5 + 0.5 * jnp.tanh(0.5 * x)


def conv_silu(raw, rim, taps):
    rows, n = raw.shape[0], rim.shape[0]
    padded = jnp.concatenate([rim, raw], axis=0)
    before = pltpu.roll(padded, 1, 0)
    old = pltpu.roll(taps[1:2] * padded + taps[0:1] * before, 2, 0)
    total = (taps[3:4] * padded + taps[2:3] * before + old)[n:]
    return total * sigmoid(total)


def unit(x, scale):
    return (x * (lax.rsqrt(jnp.sum(x * x, axis=-1, keepdims=True) + 1e-06) * scale)).astype(BF16)


def placed(*arrays):
    return [pltpu.with_memory_space_constraint(x, pltpu.HBM) for x in arrays]


def positions(c):
    return (
        lax.broadcasted_iota(jnp.int32, (c, c), 0),
        lax.broadcasted_iota(jnp.int32, (c, c), 1),
    )


def channels(rim_ref, ref, prev_ref, taps_ref, which, sl, first):
    raw = ref[:, sl].astype(F32)
    rim = jnp.where(first, rim_ref[which, :, sl].astype(F32), prev_ref[:, sl].astype(F32))
    return conv_silu(raw, rim[-8:], taps_ref[which, :, sl])


def summary_kernel(
    rim_ref, k_ref, v_ref, kp_ref, vp_ref, dec_ref, wr_ref, taps_ref, mask_ref,
    keys_ref, fresh_ref, start_ref, summary_ref, state_ref,
):
    step = pl.program_id(0)
    c = CHUNK
    subs = k_ref.shape[0] // c
    heads = dec_ref.shape[0]
    width = k_ref.shape[1] // heads

    @pl.when(step == 0)
    def _():
        rows = lax.broadcasted_iota(jnp.int32, (width, 2 * width), 0)
        cols = lax.broadcasted_iota(jnp.int32, (width, 2 * width), 1)
        eye = jnp.where(rows == cols, 1.0, 0.0).astype(F32)
        for h in range(heads):
            state_ref[h] = eye

    ri, ci = positions(c)
    tril = jnp.where(ci <= ri, 1.0, 0.0).astype(F32)
    eye = jnp.where(ci == ri, 1.0, 0.0).astype(F32)
    first = step == 0
    dec = [dec_ref[:, s * c : (s + 1) * c] for s in range(subs)]
    wr = [wr_ref[:, s * c : (s + 1) * c] for s in range(subs)]
    cum_row = [exact(x, tril, NT) for x in dec]
    cum_col = [exact(tril, x, NT) for x in dec]
    wr_col = [exact(eye, x, NT) for x in wr]
    last = [x[:, c - 1 : c] for x in cum_row]
    log_col = [cum_col[s] + jnp.log(wr_col[s]) for s in range(subs)]
    drop_col = [-wr_col[s] * jnp.exp(cum_col[s]) for s in range(subs)]
    kout_row = [jnp.exp(last[s] - cum_row[s]) for s in range(subs)]
    last_decay = [jnp.exp(x) for x in last]

    units = [(s, h) for s in range(subs) for h in range(heads)]
    n = range(len(units))

    def lanes(h):
        return slice(h * width, (h + 1) * width)

    def row(x, i):
        s, h = units[i]
        return x[s][h : h + 1, :]

    def col(x, i):
        s, h = units[i]
        return x[s][:, h : h + 1]

    def split(x):
        return {(s, h): x[h][s * c : (s + 1) * c] for s, h in units}

    k_all = [unit(channels(rim_ref, k_ref, kp_ref, taps_ref, 1, lanes(h), first), 1.0) for h in range(heads)]
    for h in range(heads):
        keys_ref[:, lanes(h)] = k_all[h]
    k = [k_all[h][s * c : (s + 1) * c] for s, h in units]
    gram = [mm(x, x, NT) for x in k]
    low = []
    for i in n:
        decay = jnp.exp(col(log_col, i) - row(cum_row, i))
        low.append(jnp.where(ci < ri, gram[i] * decay, 0.0).astype(BF16))
    inv = [eye.astype(BF16) - x * mask_ref[0] for x in low]
    level = 1
    while (1 << level) < c:
        mask = mask_ref[level]
        inner = [mm(low[i] * mask, inv[i]).astype(BF16) for i in n]
        inv = [inv[i] - mm(inv[i], inner[i]).astype(BF16) for i in n]
        level += 1
    v_all = [channels(rim_ref, v_ref, vp_ref, taps_ref, 2, lanes(h), first).astype(BF16) for h in range(heads)]
    v = [v_all[h][s * c : (s + 1) * c] for s, h in units]
    kf = [x.astype(F32) for x in k]
    sides = [
        jnp.concatenate(
            [
                (kf[i] * col(drop_col, i)).astype(BF16),
                (v[i].astype(F32) * col(wr_col, i)).astype(BF16),
            ],
            axis=1,
        )
        for i in n
    ]
    mixed = [mm(inv[i], sides[i]) for i in n]
    k_out = [(k[i].T.astype(F32) * row(kout_row, i)).astype(BF16) for i in n]
    for s in range(subs):
        at = s * heads
        start = [state_ref[h].astype(BF16) for h in range(heads)]
        for h in range(heads):
            start_ref[s, h] = start[h]
        read = [mm(mixed[at + h][:, :width].astype(BF16), start[h]) for h in range(heads)]
        fresh = [
            jnp.concatenate(
                [read[h][:, :width], mixed[at + h][:, width:] + read[h][:, width:]], axis=1
            ).astype(BF16)
            for h in range(heads)
        ]
        for h in range(heads):
            fresh_ref[s * c : (s + 1) * c, 2 * h * width : 2 * (h + 1) * width] = fresh[h]
        both = [mm(k_out[at + h], fresh[h]) for h in range(heads)]
        for h in range(heads):
            state_ref[h] = last_decay[s][h : h + 1, :] * state_ref[h] + both[h]

    @pl.when(step == pl.num_programs(0) - 1)
    def _():
        summary_ref[...] = state_ref[...].astype(BF16)


def local_kernel(
    begin, rim_ref, q_ref, qp_ref, keys_ref, fresh_ref, start_ref, dec_ref, taps_ref, *rest
):
    local_ref, qeff_ref = rest[-2:]
    step = pl.program_id(0) + begin
    c = q_ref.shape[0]
    heads = dec_ref.shape[0]
    width = q_ref.shape[1] // heads
    ri, ci = positions(c)
    tril = jnp.where(ci <= ri, 1.0, 0.0).astype(F32)
    dec = dec_ref[...]
    cum_row = exact(dec, tril, NT)
    cum_col = exact(tril, dec, NT)
    gamma_col = jnp.exp(cum_col)
    first = step == 0
    for g in range(0, heads, GROUP):
        hs = range(g, g + GROUP)
        sls = [slice(h * width, (h + 1) * width) for h in hs]
        n = range(GROUP)
        q = [unit(channels(rim_ref, q_ref, qp_ref, taps_ref, 0, sl, first), width ** -0.5) for sl in sls]
        gram = [mm(q[i], keys_ref[:, sls[i]], NT) for i in n]
        for i in n:
            h = hs[i]
            gap = cum_col[:, h : h + 1] - cum_row[h : h + 1, :]
            scores = jnp.where(ci <= ri, gram[i] * jnp.exp(gap), 0.0).astype(BF16)
            q_in = (q[i].astype(F32) * gamma_col[:, h : h + 1]).astype(BF16)
            out = mm(
                jnp.concatenate([q_in, scores], axis=1),
                jnp.concatenate(
                    [start_ref[0, h], fresh_ref[:, 2 * h * width : 2 * (h + 1) * width]], axis=0
                ),
            )
            qeff_ref[:, sls[i]] = out[:, :width].astype(BF16)
            local_ref[:, sls[i]] = out[:, width:].astype(BF16)


def level_masks(c):
    r = np.arange(c)
    differ = r[:, None] ^ r[None, :]
    lower = r[:, None] > r[None, :]
    levels = []
    size = 1
    while size < c:
        levels.append(lower & (differ >= size) & (differ < 2 * size))
        size *= 2
    return jnp.asarray(np.stack(levels), BF16)


def front(rim, query_raw, key_raw, value_raw, log_decay, write_strength, conv_weight):
    rows, channel_count = query_raw.shape
    heads = log_decay.shape[0]
    width = channel_count // heads
    c = CHUNK
    steps = rows // c
    per = c // RIM
    masks = level_masks(c)
    block = pl.BlockSpec((c, channel_count), lambda i: (i, 0))
    wide = pl.BlockSpec((c, 2 * channel_count), lambda i: (i, 0))
    prev = pl.BlockSpec((RIM, channel_count), lambda i: (jnp.maximum(i * per - 1, 0), 0))
    gates = pl.BlockSpec((heads, c), lambda i: (0, i))
    rims = pl.BlockSpec((3, RIM, channel_count), lambda i: (0, 0, 0))
    taps = pl.BlockSpec((3, 4, channel_count), lambda i: (0, 0, 0))
    starts = pl.BlockSpec((1, heads, width, 2 * width), lambda i: (i, 0, 0, 0))
    params = pltpu.CompilerParams(vmem_limit_bytes=48 << 20)
    subs = SUBS if steps % SUBS == 0 else 1
    big = pl.BlockSpec((subs * c, channel_count), lambda i: (i, 0))
    keys, fresh, start, summary = pl.pallas_call(
        summary_kernel,
        grid=(steps // subs,),
        in_specs=[
            rims, big, big,
            pl.BlockSpec((RIM, channel_count), lambda i: (jnp.maximum(i * per * subs - 1, 0), 0)),
            pl.BlockSpec((RIM, channel_count), lambda i: (jnp.maximum(i * per * subs - 1, 0), 0)),
            pl.BlockSpec((heads, subs * c), lambda i: (0, i)),
            pl.BlockSpec((heads, subs * c), lambda i: (0, i)), taps,
            pl.BlockSpec(masks.shape, lambda i: (0, 0, 0)),
        ],
        out_specs=[
            big,
            pl.BlockSpec((subs * c, 2 * channel_count), lambda i: (i, 0)),
            pl.BlockSpec((subs, heads, width, 2 * width), lambda i: (i, 0, 0, 0)),
            pl.BlockSpec((heads, width, 2 * width), lambda i: (0, 0, 0)),
        ],
        out_shape=[
            pltpu.HBM((rows, channel_count), BF16),
            pltpu.HBM((rows, 2 * channel_count), BF16),
            pltpu.HBM((steps, heads, width, 2 * width), BF16),
            jax.ShapeDtypeStruct((heads, width, 2 * width), BF16),
        ],
        scratch_shapes=[pltpu.VMEM((heads, width, 2 * width), F32)],
        compiler_params=params,
        name="summary",
    )(rim, *placed(key_raw, value_raw, key_raw, value_raw, log_decay, write_strength, conv_weight, masks))
    first = steps // 3

    def local_part(begin, count, done, rim, keys, fresh, start):
        def at(spec):
            return pl.BlockSpec(spec.block_shape, lambda i: spec.index_map(i + begin))

        return pl.pallas_call(
            functools.partial(local_kernel, begin),
            grid=(count,),
            in_specs=[rims, *map(at, (block, prev, block, wide, starts, gates)), taps]
            + [pl.BlockSpec(memory_space=pl.ANY)] * len(done),
            out_specs=[at(block), at(block)],
            out_shape=[
                pltpu.HBM((rows, channel_count), BF16),
                pltpu.HBM((rows, channel_count), BF16),
            ],
            input_output_aliases={8 + i: i for i in range(len(done))},
            compiler_params=params,
            name="local",
        )(rim, *placed(query_raw, query_raw, keys, fresh, start, log_decay, conv_weight, *done))

    def early():
        return local_part(0, first, (), rim, keys, fresh, start)

    def late(done):
        return local_part(first, steps - first, done, rim, keys, fresh, start)

    return early, late, summary


def out_kernel(
    info_ref, state_ref, local_ref, qeff_ref, gate_ref, gain_ref, weight_ref, *out_refs
):
    step = pl.program_id(0)
    heads, width = state_ref.shape[0], state_ref.shape[1]
    rows = local_ref.shape[0]
    base = info_ref[0] + info_ref[2 + step] * rows
    valid = base + lax.broadcasted_iota(jnp.int32, (rows, width), 0) < info_ref[1]
    gated = []
    for h in range(heads):
        sl = slice(h * width, (h + 1) * width)
        o = local_ref[:, sl].astype(F32) + mm(qeff_ref[:, sl], state_ref[h])
        norm = lax.rsqrt(jnp.mean(o * o, axis=-1, keepdims=True) + 1e-06)
        g = gate_ref[:, sl].astype(F32)
        o = o * norm * gain_ref[...] * (g * sigmoid(g))
        gated.append(jnp.where(valid, o, 0.0).astype(BF16))
    result = mm(jnp.concatenate(gated, axis=1), weight_ref[...]).astype(BF16)
    for i, out_ref in enumerate(out_refs):

        @pl.when(step == i)
        def _(out_ref=out_ref):
            out_ref[...] = result


def passed_along(block, axis, distance):
    devices = range(lax.axis_size(axis))
    route = [(i - distance, i) for i in devices if i - distance in devices]
    return lax.ppermute(block, axis, route)


def ends_kernel(q_ref, k_ref, v_ref, out_ref):
    out_ref[0] = q_ref[...]
    out_ref[1] = k_ref[...]
    out_ref[2] = v_ref[...]


def ends(*arrays):
    rows, channel_count = arrays[0].shape
    last = rows // RIM - 1
    return pl.pallas_call(
        ends_kernel,
        grid=(1,),
        in_specs=[pl.BlockSpec((RIM, channel_count), lambda i: (last, 0))] * 3,
        out_specs=pl.BlockSpec((3, RIM, channel_count), lambda i: (0, 0, 0)),
        out_shape=jax.ShapeDtypeStruct((3, RIM, channel_count), BF16),
        name="ends",
    )(*placed(*arrays))


def carried_in(summary, axis, early, late):
    width = summary.shape[1]
    count = lax.axis_size(axis)
    move, own = summary[:, :, :width], summary[:, :, width:]

    def apply(a, b, s):
        return jnp.einsum("hij,hjk->hik", a, s, preferred_element_type=F32) + b.astype(F32)

    if count == 4:
        first = lax.ppermute(own, axis, [(0, 1)])
        third = lax.ppermute(summary, axis, [(2, 3)])
        done = early()
        first, done = lax.optimization_barrier((first, done))
        pair = apply(move, own, first).astype(BF16)
        far = lax.ppermute(pair, axis, [(1, 3)])
        near = lax.ppermute(pair, axis, [(1, 2)])
        done, pair = lax.optimization_barrier((done, pair))
        done = late(done)
        state = apply(third[:, :, :width], third[:, :, width:], far)
        return (state + near.astype(F32) + first.astype(F32)).astype(BF16), *done
    state = passed_along(own, axis, 1)
    for _ in range(count - 2):
        state = passed_along(apply(move, own, state).astype(BF16), axis, 1)
    return state, *late(early())


def on_device(
    query_raw, key_raw, value_raw, out_gate, log_decay, write_strength,
    conv_weight, norm_gain, out_weight, history_end,
):
    rows, channel_count = query_raw.shape
    heads = log_decay.shape[0]
    width = channel_count // heads
    rim = passed_along(ends(query_raw, key_raw, value_raw), "seq", 1)
    early, late, summary = front(
        rim, query_raw, key_raw, value_raw, log_decay, write_strength, conv_weight
    )
    state, local, qeff = carried_in(summary, "seq", early, late)
    owners = lax.axis_size("head")
    mine = lax.axis_index("head")
    dim = out_weight.shape[1]
    start = lax.axis_index("seq") * rows
    gain = norm_gain.reshape(1, width)

    def partial(*blocks, after=None, resident=False):
        tile = rows // owners
        info = jnp.stack([start, history_end[0], *blocks]).astype(jnp.int32)
        if after is not None:
            info, after = lax.optimization_barrier((info, after))
        tiles = pl.BlockSpec((tile, channel_count), lambda i, s: (s[2 + i], 0))
        weight = out_weight if resident else placed(out_weight)[0]
        return pl.pallas_call(
            out_kernel,
            grid_spec=pltpu.PrefetchScalarGridSpec(
                num_scalar_prefetch=1,
                grid=(len(blocks),),
                in_specs=[
                    pl.BlockSpec((heads, width, width), lambda i, s: (0, 0, 0)),
                    tiles, tiles, tiles,
                    pl.BlockSpec((1, width), lambda i, s: (0, 0)),
                    pl.BlockSpec(memory_space=pltpu.VMEM)
                    if resident
                    else pl.BlockSpec((channel_count, dim), lambda i, s: (0, 0)),
                ],
                out_specs=[pl.BlockSpec((tile, dim), lambda i, s: (0, 0))] * len(blocks),
            ),
            out_shape=[jax.ShapeDtypeStruct((tile, dim), BF16)] * len(blocks),
            compiler_params=pltpu.CompilerParams(vmem_limit_bytes=24 << 20),
            name="outputs",
        )(info, state, *placed(local, qeff, out_gate, gain), weight)

    def exchange(block, bit):
        return lax.ppermute(block, "head", [(i, i ^ bit) for i in range(owners)])

    def added(a, b):
        return (a.astype(F32) + b.astype(F32)).astype(BF16)

    if owners != 4:
        blocks = jnp.concatenate(partial(*range(owners)), axis=0)
        return lax.psum_scatter(blocks, "head", scatter_dimension=0, tiled=True)
    sent, kept = partial(mine ^ 3, mine ^ 2, resident=True)
    far = added(kept, exchange(sent, 1))
    far_got = exchange(far, 2)
    sent, kept = partial(mine ^ 1, mine, after=far)
    near = kept.astype(F32) + exchange(sent, 1).astype(F32)
    return (near + far_got.astype(F32)).astype(BF16)


def solution(mesh):
    return jax.shard_map(
        on_device,
        mesh=mesh,
        in_specs=(
            P(("parts", "seq"), "head"),
            P(("parts", "seq"), "head"),
            P(("parts", "seq"), "head"),
            P(("parts", "seq"), "head"),
            P("head", ("parts", "seq")),
            P("head", ("parts", "seq")),
            P(None, None, "head"),
            P(),
            P("head", None),
            P("parts"),
        ),
        out_specs=P(("parts", "seq", "head"), None),
        check_vma=False,
    )
```
